32 devices in a mesh: actors: 8 (over z, y), rep: 4 (over x, core).
Axes of the slice: x: 2, y: 2, z: 4, core: 2. Of those that a mesh axis runs over, the one named last changes fastest.
Arguments:
- features: bfloat16 [4, 8, 16, 1024], P('rep', 'actors'), may hold values from -6 to 6
- rewards: float32 [4, 8, 16], P('rep', 'actors'), may hold values from -2 to 6, as said below
- lengths: int32 [4, 8, 8], P('rep', 'actors'), may hold values from 1 to 3, 16 in all within a row
- owners: int32 [4, 8, 8], P('rep', 'actors'), may hold values from 0 to 7, each once within a row
- norm_gain: float32 [1024], replicated, may hold values from 0.4 to 1.6
Outputs:
- trainer_rows: bfloat16 [4, 8, 24, 1024], P('rep', 'actors')
- trainer_rewards: float32 [4, 8, 24], P('rep', 'actors')
- trainer_counts: int32 [8], P('actors')
The draws below stay inside these ranges and needn't reach their ends.
Inputs may be any that keep to these rules, and one draw needn't show every extreme that they name: `rewards`: rewards of each actor are centered on a level that differs from actor to actor.
All inputs are finite; a program needn't handle non-finite values.
Results may differ from the reference program's by a relative error of at most 0.0004.
Values may be sent and summed in bfloat16 or wider, within the bound.
No kernel may reach another device: no remote copies, remote signals or barrier semaphores. Data moves between devices by JAX's collectives and lax.ppermute only.
A program may use at most 64 MiB of HBM per device.

```python
import math
import jax
import jax.numpy as jnp
import numpy as np
from jax import lax

F = 1024
GAMES = 8
ROWS_DEV = 16
CAP = 3
N_ACTORS = 8
N_REP = 4


def draw_rewards(key, part):
    shape = (N_REP, N_ACTORS, ROWS_DEV)
    device_pos = (jnp.arange(N_REP)[:, None, None] * N_ACTORS + jnp.arange(N_ACTORS)[None, :, None]).astype(jnp.float32)
    level = 1.0 + 2.0 * device_pos / (N_REP * N_ACTORS - 1)
    noise = jnp.clip(jax.random.normal(jax.random.fold_in(key, 3), shape, jnp.float32), -3.0, 3.0)
    return (level + noise).astype(jnp.float32)


def steps_of(key, extent, cuts, smallest, top_value):
    loudness, own = 1.0, jax.random.fold_in(key, 6)
    for axis_at, shards_of in cuts:
        steps = jnp.exp(jax.random.uniform(jax.random.fold_in(own, axis_at), (shards_of,), jnp.float32, smallest / len(cuts), top_value / len(cuts)))
        loudness = loudness * jnp.repeat(steps, extent[axis_at] // shards_of).reshape([-1 if axis == axis_at else 1 for axis in range(len(extent))])
    return loudness


def profile(number_of, total, reach, skew):
    weights = [(1 << 20) // math.isqrt(standing ** skew) + 1 for standing in range(2, number_of + 1)]
    spare, given = total - reach - (number_of - 1), [1] * (number_of - 1)
    while spare > 0:
        movable = [i for i in range(number_of - 1) if given[i] < reach]
        mass, budget = sum([weights[i] for i in movable]), spare
        for i in movable:
            addition = min(reach - given[i], max(1, budget * weights[i] // mass), spare)
            given[i] = given[i] + addition
            spare = spare - addition
    return np.array([reach] + given)


def uneven(stream_key, count, total, reach, slope):
    if count == 2:
        one = jax.random.randint(stream_key, (), max(1, total - reach), min(reach, total - 1) + 1)
        return jnp.stack([one, total - one])
    sizes = jnp.asarray(profile(count, total, reach, slope), jnp.int32)
    couples = (count - 1) // 2
    giver, receiver = sizes[1:1 + 2 * couples:2], sizes[2:2 + 2 * couples:2]
    slack = jnp.minimum(giver - 1, reach - receiver)
    shifted = jax.random.randint(jax.random.fold_in(stream_key, 1), (couples,), 0, 1 << 20) % (slack + 1)
    sizes = sizes.at[1:1 + 2 * couples:2].set(giver - shifted).at[2:2 + 2 * couples:2].set(receiver + shifted)
    return sizes[jax.random.permutation(jax.random.fold_in(stream_key, 2), count)]


def bell_draw(rng, extent, spread, most, cuts=(), kind=jnp.bfloat16):
    factor_of = steps_of(rng, extent, cuts, -0.22, 0.18) if cuts else 1.0
    values = jax.random.normal(rng, extent, jnp.float32) * spread * factor_of
    return jnp.minimum(jnp.maximum(values, -most), most).astype(kind)


def setup_inputs(seed: int = 0) -> dict:
    streams_of = jax.random.split(jax.random.key(seed), 6)
    features = bell_draw(streams_of[0], (N_REP, N_ACTORS, ROWS_DEV, F), 1.0, 6.0, ((0, 4), (1, 8)))
    rewards = draw_rewards(jax.random.fold_in(streams_of[5], 71), 0)
    lengths = jax.vmap(lambda own: uneven(own, GAMES, ROWS_DEV, CAP, 2))(jax.random.split(streams_of[2], N_REP * N_ACTORS)).reshape((N_REP, N_ACTORS, GAMES)).astype(jnp.int32)
    owners = jax.vmap(lambda own: jax.random.permutation(own, GAMES))(jax.random.split(streams_of[3], N_REP * N_ACTORS)).reshape((N_REP, N_ACTORS, GAMES)).astype(jnp.int32)
    norm_gain = jnp.clip(1.0 + 0.12 * jax.random.normal(streams_of[4], (F,), jnp.float32), 0.4, 1.6)
    return {"features": features, "rewards": rewards, "lengths": lengths, "owners": owners, "norm_gain": norm_gain}


EPS_NORM = 1e-06
EPS_VAR = 1e-05

def rms_scale(rows, norm_gain):
    widened = rows.astype(jnp.float32)
    square_mean = lax.optimization_barrier(jnp.mean(widened * widened, axis=-1, keepdims=True))
    return (widened * lax.rsqrt(square_mean + EPS_NORM) * norm_gain).astype(jnp.bfloat16)

def reference(features, rewards, lengths, owners, norm_gain):
    row_total = N_REP * N_ACTORS * ROWS_DEV
    reward_mean = jnp.sum(rewards) / row_total
    second = jnp.sum(rewards * rewards) / row_total
    inv_spread = lax.rsqrt(second - reward_mean * reward_mean + EPS_VAR)
    starts = jnp.cumsum(lengths, axis=-1) - lengths
    trainer_ids = jnp.arange(GAMES, dtype=jnp.int32)
    owns_game = (owners[..., None, :] == trainer_ids[:, None]).astype(jnp.int32)
    held_len = lax.optimization_barrier(jnp.sum(owns_game * lengths[..., None, :], axis=-1))
    held_start = lax.optimization_barrier(jnp.sum(owns_game * starts[..., None, :], axis=-1))
    slot_pos = jnp.arange(CAP, dtype=jnp.int32)
    usable = slot_pos < held_len[..., None]
    row_index = jnp.minimum(held_start[..., None] + slot_pos, ROWS_DEV - 1).astype(jnp.int32)
    scaled_rewards = (rewards - reward_mean) * inv_spread

    def one_group(group):
        group_feats, group_rews, group_index, group_keep = group
        normed = rms_scale(group_feats, norm_gain)
        picked = jax.vmap(lambda block_rows, picks: jnp.take(block_rows, picks, axis=0))(normed, group_index)
        picked = jnp.where(group_keep[..., None], picked, jnp.zeros((), jnp.bfloat16))
        picked_rew = jax.vmap(lambda block_rows, picks: jnp.take(block_rows, picks, axis=0))(group_rews, group_index)
        picked_rew = jnp.where(group_keep, picked_rew, jnp.zeros((), jnp.float32))
        rows_done = picked.transpose(1, 0, 2, 3).reshape(GAMES, GAMES * CAP, F)
        rews_done = picked_rew.transpose(1, 0, 2).reshape(GAMES, GAMES * CAP)
        return (rows_done, rews_done)
    rows_out, rews_out = lax.map(one_group, (features, scaled_rewards, row_index, usable))
    counts = lax.optimization_barrier(jnp.sum(held_len, axis=(0, 1))).astype(jnp.int32)
    return (rows_out, rews_out, counts)
```

```python
import functools

import jax
import jax.numpy as jnp
from jax import lax
from jax.experimental import pallas as pl
from jax.experimental.pallas import tpu as pltpu
from jax.sharding import PartitionSpec as P

CAP = 3
EPS_NORM = 1e-06
EPS_VAR = 1e-05

LANES = 128
LEN_AT, SUM_AT, SQUARE_AT = CAP, CAP + 1, CAP + 2
BLOCK = 8
SCALARS = 2 * CAP


def pack_kernel(groups, length_ref, owner_ref, rows_ref, gain_ref, reward_ref, out_ref, start_of, length_of):
    games = length_ref.shape[1]
    row_count, width = rows_ref.shape
    half = width // 2
    mine = lax.axis_index("rep")

    start = jnp.int32(0)
    for game in range(games):
        size = length_ref[0, game]
        owner = owner_ref[0, game]
        start_of[owner] = start
        length_of[owner] = size
        start = start + size

    padded = -(-games // 16) * 16
    trainer = lax.broadcasted_iota(jnp.int32, (padded, LANES), 0)
    lane = lax.broadcasted_iota(jnp.int32, (padded, LANES), 1)
    first = jnp.zeros((padded, LANES), jnp.int32)
    size = jnp.zeros((padded, LANES), jnp.int32)
    for t in range(games):
        first = jnp.where(trainer == t, start_of[t], first)
        size = jnp.where(trainer == t, length_of[t], size)
    reward = reward_ref[...]
    spread = jnp.broadcast_to(reward, (padded, row_count))
    at = lax.broadcasted_iota(jnp.int32, (padded, row_count), 1)
    values = jnp.where(lane == LEN_AT, size.astype(jnp.float32), 0.0)
    values = jnp.where(lane == SUM_AT, jnp.sum(reward, axis=1, keepdims=True), values)
    values = jnp.where(lane == SQUARE_AT, jnp.sum(reward * reward, axis=1, keepdims=True), values)
    for j in range(CAP):
        here = (at == first[:, :row_count] + j) & (size[:, :row_count] > j)
        values = jnp.where(lane == j, jnp.sum(jnp.where(here, spread, 0.0), axis=1, keepdims=True), values)
    high = values.astype(jnp.bfloat16)
    rest = values - high.astype(jnp.float32)
    middle = rest.astype(jnp.bfloat16)
    low = (rest - middle.astype(jnp.float32)).astype(jnp.bfloat16)
    scalars = jnp.concatenate(
        [high, middle, low, jnp.zeros((padded, half - 3 * LANES), jnp.bfloat16)], axis=1
    )

    wide = rows_ref[...].astype(jnp.float32)
    square_mean = jnp.sum(wide * wide, axis=1, keepdims=True) / width
    normed = (wide * lax.rsqrt(square_mean + EPS_NORM) * gain_ref[...]).astype(jnp.bfloat16)
    source = jnp.concatenate([normed[:, :half], normed[:, half:], scalars], axis=0)

    depth = 2 * row_count + padded
    chunk = groups * BLOCK
    i = lax.broadcasted_iota(jnp.int32, (chunk, depth), 0)
    column = lax.broadcasted_iota(jnp.int32, (chunk, depth), 1)
    group, q = i // BLOCK, i % BLOCK
    j = q // 2
    held = (q < SCALARS) & (group == mine)
    offset = j + (q % 2) * row_count
    limit = jnp.where(held, j, row_count)
    for t in range(games):
        wanted = jnp.where(limit < length_of[t], offset + start_of[t], -1)
        wanted = jnp.where(q == SCALARS, 2 * row_count + t, wanted)
        pick = jnp.where(column == wanted, 1.0, 0.0).astype(jnp.bfloat16)
        out_ref[t * chunk : (t + 1) * chunk, :] = jnp.dot(
            pick, source, preferred_element_type=jnp.float32
        ).astype(jnp.bfloat16)


def unpack_kernel(groups, rows_total, in_ref, rows_ref, reward_ref, count_ref):
    depth, half = in_ref.shape
    slots = rows_ref.shape[0]
    actors = slots // CAP
    mine = lax.axis_index("rep")
    blocks = in_ref[...]

    slot = lax.broadcasted_iota(jnp.int32, (slots, depth), 0)
    column = lax.broadcasted_iota(jnp.int32, (slots, depth), 1)
    at = ((slot // CAP) * groups + mine) * BLOCK + 2 * (slot % CAP)
    left = jnp.where(column == at, 1.0, 0.0)
    right = jnp.where(column == at + 1, 1.0, 0.0)
    source = lax.broadcasted_iota(jnp.int32, (actors, depth), 0)
    column = lax.broadcasted_iota(jnp.int32, (actors, depth), 1)
    own = jnp.where(column == (source * groups + mine) * BLOCK + SCALARS, 1.0, 0.0)
    every = jnp.where(column % BLOCK == SCALARS, 1.0, 0.0)
    pick = jnp.concatenate([left, right, own, every], axis=0).astype(jnp.bfloat16)
    got = jnp.dot(pick, blocks, preferred_element_type=jnp.float32)

    rows_ref[:, :half] = got[:slots].astype(jnp.bfloat16)
    rows_ref[:, half:] = got[slots : 2 * slots].astype(jnp.bfloat16)
    scalars = got[2 * slots :, :LANES] + got[2 * slots :, LANES : 2 * LANES] + got[2 * slots :, 2 * LANES : 3 * LANES]
    own, every = scalars[:actors], scalars[actors : 2 * actors]
    mean = every[:, SUM_AT : SUM_AT + 1] / rows_total
    second = every[:, SQUARE_AT : SQUARE_AT + 1] / rows_total
    scale = lax.rsqrt(second - mean * mean + EPS_VAR)
    lane = lax.broadcasted_iota(jnp.int32, (actors, LANES), 1)
    source = lax.broadcasted_iota(jnp.int32, (actors, LANES), 0)
    size = own[:, LEN_AT : LEN_AT + 1]
    placed = jnp.zeros((actors, LANES), jnp.float32)
    for j in range(CAP):
        value = jnp.where(size > j, (own[:, j : j + 1] - mean) * scale, 0.0)
        placed = jnp.where(lane == source * CAP + j, value, placed)
    reward_ref[...] = jnp.sum(placed, axis=0, keepdims=True)[:, :slots]
    count_ref[...] = every[:1, LEN_AT : LEN_AT + 1].astype(jnp.int32)


def fused(features, rewards, lengths, owners, norm_gain):
    row_count, width = features.shape[2:]
    games = lengths.shape[2]
    actors, groups = lax.axis_size("actors"), lax.axis_size("rep")
    half = width // 2
    vmem = pl.BlockSpec(memory_space=pltpu.VMEM)
    smem = pl.BlockSpec(memory_space=pltpu.SMEM)
    packed = pl.pallas_call(
        functools.partial(pack_kernel, groups),
        out_shape=jax.ShapeDtypeStruct((games * groups * BLOCK, half), jnp.bfloat16),
        in_specs=[smem, smem, vmem, vmem, vmem],
        out_specs=vmem,
        scratch_shapes=[pltpu.SMEM((games,), jnp.int32), pltpu.SMEM((games,), jnp.int32)],
        name="pack",
    )(
        lengths.reshape(1, games),
        owners.reshape(1, games),
        features.reshape(row_count, width),
        norm_gain.reshape(1, width),
        rewards.reshape(1, row_count),
    )
    landed = lax.all_to_all(packed, ("actors", "rep"), split_axis=0, concat_axis=0, tiled=True)
    rows, scaled, count = pl.pallas_call(
        functools.partial(unpack_kernel, groups, row_count * actors * groups),
        out_shape=(
            jax.ShapeDtypeStruct((actors * CAP, width), jnp.bfloat16),
            jax.ShapeDtypeStruct((1, actors * CAP), jnp.float32),
            jax.ShapeDtypeStruct((1, 1), jnp.int32),
        ),
        in_specs=[vmem],
        out_specs=(vmem, vmem, vmem),
        name="unpack",
    )(landed)
    return (rows.reshape(1, 1, -1, width), scaled.reshape(1, 1, -1), count.reshape(1))


def rms_scale(rows, norm_gain):
    widened = rows.astype(jnp.float32)
    square_mean = jnp.mean(widened * widened, axis=-1, keepdims=True)
    return (widened * lax.rsqrt(square_mean + EPS_NORM) * norm_gain).astype(jnp.bfloat16)


def plain(features, rewards, lengths, owners, norm_gain):
    rows_here = features[0, 0]
    reward_here = rewards[0, 0]
    game_len = lengths[0, 0]
    game_owner = owners[0, 0]
    games = game_len.shape[0]
    row_count = rows_here.shape[0]
    width = rows_here.shape[1]
    row_total = row_count * lax.axis_size("actors") * lax.axis_size("rep")
    starts = jnp.cumsum(game_len) - game_len
    trainer_ids = jnp.arange(games, dtype=jnp.int32)
    owns_game = (game_owner[None, :] == trainer_ids[:, None]).astype(jnp.int32)
    held_len = jnp.sum(owns_game * game_len[None, :], axis=1)
    held_start = jnp.sum(owns_game * starts[None, :], axis=1)
    slot_pos = jnp.arange(CAP, dtype=jnp.int32)
    usable = slot_pos[None, :] < held_len[:, None]
    row_index = jnp.minimum(held_start[:, None] + slot_pos[None, :], row_count - 1)
    outgoing = jnp.where(usable, jnp.take(reward_here, row_index, axis=0), jnp.zeros((), jnp.float32))
    outgoing = jnp.concatenate([outgoing, held_len.astype(jnp.float32)[:, None]], axis=1)
    arrived = lax.all_to_all(outgoing, "actors", split_axis=0, concat_axis=0, tiled=True)
    arrived, arrived_len = arrived[:, :CAP], arrived[:, CAP:]
    normed = rms_scale(rows_here, norm_gain)
    packed = jnp.where(usable[:, :, None], jnp.take(normed, row_index, axis=0), jnp.zeros((), jnp.bfloat16))
    landed = lax.all_to_all(packed, "actors", split_axis=0, concat_axis=0, tiled=True)
    first, second = lax.psum((jnp.sum(arrived), jnp.sum(arrived * arrived)), ("actors", "rep"))
    reward_mean = first / row_total
    inv_spread = lax.rsqrt(second / row_total - reward_mean * reward_mean + EPS_VAR)
    keep_slot = slot_pos[None, :].astype(jnp.float32) < arrived_len
    scaled = jnp.where(keep_slot, (arrived - reward_mean) * inv_spread, jnp.zeros((), jnp.float32))
    count_here = jnp.sum(arrived_len).astype(jnp.int32)
    counts = lax.psum(count_here, "rep")
    return (landed.reshape(1, 1, -1, width), scaled.reshape(1, 1, -1), counts.reshape(1))


def local(features, rewards, lengths, owners, norm_gain):
    actors, groups = lax.axis_size("actors"), lax.axis_size("rep")
    width = features.shape[3]
    fits = actors * CAP <= LANES and actors % 8 == 0 and width % 1024 == 0 and features.shape[2] % 16 == 0
    step = fused if fits else plain
    return step(features, rewards, lengths, owners, norm_gain)


def solution(mesh):
    return jax.shard_map(
        local,
        mesh=mesh,
        in_specs=(
            P("rep", "actors", None, None),
            P("rep", "actors", None),
            P("rep", "actors", None),
            P("rep", "actors", None),
            P(),
        ),
        out_specs=(P("rep", "actors", None, None), P("rep", "actors", None), P("actors")),
        check_vma=False,
    )
```

```python
import functools

import jax
import jax.numpy as jnp
from jax import lax
from jax.experimental import pallas as pl
from jax.experimental.pallas import tpu as pltpu
from jax.sharding import PartitionSpec as P

CAP = 3
EPS_NORM = 1e-06
EPS_VAR = 1e-05

LANES = 128
SUBLANES = 8
VMEM_GRANT = 8 << 20
HIGH, MIDDLE, LOW, KEPT = range(4)


def pack_kernel(
    groups, length_hbm, owner_hbm, rows_hbm, gain_hbm, reward_hbm, out_ref,
    length_ref, owner_ref, rows_ref, gain_ref, reward_ref, reward_at, start_of, length_of, sems,
):
    games = length_ref.shape[1]
    row_count, width = rows_ref.shape
    columns = out_ref.shape[2] // LANES - 1
    across = width // LANES
    copies = [
        pltpu.make_async_copy(source, target, sems.at[n])
        for n, (source, target) in enumerate(
            (
                (length_hbm, length_ref),
                (owner_hbm, owner_ref),
                (rows_hbm, rows_ref),
                (gain_hbm, gain_ref),
                (reward_hbm, reward_ref),
                (reward_hbm, reward_at),
            )
        )
    ]
    for copy in copies:
        copy.start()
    mine, actor = lax.axis_index("rep"), lax.axis_index("actors")
    actors = lax.axis_size("actors")
    lane = lax.broadcasted_iota(jnp.int32, (SUBLANES, LANES), 1)
    sublane = lax.broadcasted_iota(jnp.int32, (SUBLANES, LANES), 0)
    for copy in copies:
        copy.wait()

    start = jnp.int32(0)
    for game in range(games):
        owner = owner_ref[0, game]
        start_of[owner] = start
        length_of[owner] = length_ref[0, game]
        start = start + length_ref[0, game]

    wide = rows_ref[...].astype(jnp.float32)
    square_mean = jnp.sum(wide * wide, axis=1, keepdims=True) / width
    normed = (wide * lax.rsqrt(square_mean + EPS_NORM) * gain_ref[...]).astype(jnp.bfloat16)
    source = jnp.concatenate([normed[:, k * LANES : (k + 1) * LANES] for k in range(across)], axis=0)
    lanes_of = lax.broadcasted_iota(jnp.int32, (SUBLANES, across * row_count), 1)
    rows_of = lax.broadcasted_iota(jnp.int32, (SUBLANES, across * row_count), 0)
    picks = []
    for c in range(columns):
        piece = rows_of * columns + c
        position = piece // across
        base = lanes_of - (piece % across) * row_count - position
        for t in range(games):
            hit = (base == start_of[t]) & (position < length_of[t])
            picks.append(jnp.where(hit, 1.0, 0.0))
    picked = jnp.dot(
        jnp.concatenate(picks, axis=0).astype(jnp.bfloat16), source, preferred_element_type=jnp.float32
    ).astype(jnp.bfloat16)
    for c in range(columns):
        for t in range(games):
            at = (c * games + t) * SUBLANES
            out_ref[t * groups + mine, :, c * LANES : (c + 1) * LANES] = picked[at : at + SUBLANES]

    reward = reward_ref[...]
    first = jnp.sum(reward, axis=1, keepdims=True)
    second = jnp.sum(reward * reward, axis=1, keepdims=True)
    common = jnp.where(lane == CAP * actors, first, jnp.where(lane == CAP * actors + 1, second, 0.0))
    for t in range(games):
        begin, size = start_of[t], length_of[t]
        values = jnp.where(lane == CAP * actors + 2, size.astype(jnp.float32), common)
        for j in range(CAP):
            value = jnp.where(j < size, reward_at[0, jnp.minimum(begin + j, row_count - 1)], 0.0)
            values = jnp.where(lane == CAP * actor + j, value, values)
        high = values.astype(jnp.bfloat16).astype(jnp.float32)
        middle = (values - high).astype(jnp.bfloat16).astype(jnp.float32)
        low = values - high - middle
        kept = jnp.where((lane >= CAP * actor) & (lane < CAP * actor + size), 1.0, 0.0)
        tile = jnp.where(sublane == HIGH, high, 0.0)
        tile = jnp.where(sublane == MIDDLE, middle, tile)
        tile = jnp.where(sublane == LOW, low, tile)
        tile = jnp.where(sublane == KEPT, kept, tile).astype(jnp.bfloat16)
        for group in range(groups):
            out_ref[t * groups + group, :, columns * LANES :] = tile


def unpack_kernel(groups, rows_total, in_ref, rows_hbm, reward_hbm, count_hbm, rows_ref, reward_ref, count_ref, sems):
    actors = in_ref.shape[0] // groups
    columns = in_ref.shape[2] // LANES - 1
    slots, width = rows_ref.shape
    across = width // LANES
    mine = lax.axis_index("rep")

    depth = columns * actors * SUBLANES
    pieces = jnp.concatenate(
        [in_ref[s * groups + mine, :, c * LANES : (c + 1) * LANES] for c in range(columns) for s in range(actors)],
        axis=0,
    )
    slot = lax.broadcasted_iota(jnp.int32, (slots, depth), 0)
    column = lax.broadcasted_iota(jnp.int32, (slots, depth), 1)
    actor, q = (column // SUBLANES) % actors, column % SUBLANES
    piece = q * columns + column // (SUBLANES * actors)
    piece = jnp.where(slot // CAP == actor, piece - (slot % CAP) * across, -1)
    pick = jnp.concatenate([jnp.where(piece == k, 1.0, 0.0) for k in range(across)], axis=0)
    got = jnp.dot(pick.astype(jnp.bfloat16), pieces, preferred_element_type=jnp.float32).astype(jnp.bfloat16)
    for k in range(across):
        rows_ref[:, k * LANES : (k + 1) * LANES] = got[k * slots : (k + 1) * slots]
    rows_copy = pltpu.make_async_copy(rows_ref, rows_hbm, sems.at[0])
    rows_copy.start()

    def tile(block):
        return in_ref[block, :, columns * LANES :].astype(jnp.float32)

    own = sum(tile(s * groups + mine) for s in range(actors))
    every = sum(tile(block) for block in range(actors * groups))
    own_value = own[HIGH : HIGH + 1] + own[MIDDLE : MIDDLE + 1] + own[LOW : LOW + 1]
    every_value = every[HIGH : HIGH + 1] + every[MIDDLE : MIDDLE + 1] + every[LOW : LOW + 1]
    mean = every_value[:, slots : slots + 1] / rows_total
    second = every_value[:, slots + 1 : slots + 2] / rows_total
    scale = lax.rsqrt(second - mean * mean + EPS_VAR)
    scaled = jnp.where(own[KEPT : KEPT + 1] > 0.5, (own_value - mean) * scale, 0.0)
    reward_ref[...] = scaled[:, :slots]
    count_ref[...] = every_value[:, slots + 2 : slots + 3].astype(jnp.int32)
    reward_copy = pltpu.make_async_copy(reward_ref, reward_hbm, sems.at[1])
    count_copy = pltpu.make_async_copy(count_ref, count_hbm, sems.at[2])
    reward_copy.start()
    count_copy.start()
    rows_copy.wait()
    reward_copy.wait()
    count_copy.wait()


def fused(features, rewards, lengths, owners, norm_gain):
    row_count, width = features.shape[2:]
    games = lengths.shape[2]
    actors, groups = lax.axis_size("actors"), lax.axis_size("rep")
    slots = actors * CAP
    columns = CAP * width // (SUBLANES * LANES)
    vmem = pl.BlockSpec(memory_space=pltpu.VMEM)
    hbm = pl.BlockSpec(memory_space=pltpu.HBM)
    packed = pl.pallas_call(
        functools.partial(pack_kernel, groups),
        out_shape=jax.ShapeDtypeStruct((games * groups, SUBLANES, (columns + 1) * LANES), jnp.bfloat16),
        in_specs=[hbm] * 5,
        out_specs=vmem,
        scratch_shapes=[
            pltpu.SMEM((1, games), jnp.int32),
            pltpu.SMEM((1, games), jnp.int32),
            pltpu.VMEM((row_count, width), jnp.bfloat16),
            pltpu.VMEM((1, width), jnp.float32),
            pltpu.VMEM((1, row_count), jnp.float32),
            pltpu.SMEM((1, row_count), jnp.float32),
            pltpu.SMEM((games,), jnp.int32),
            pltpu.SMEM((games,), jnp.int32),
            pltpu.SemaphoreType.DMA((6,)),
        ],
        compiler_params=pltpu.CompilerParams(vmem_limit_bytes=VMEM_GRANT),
        name="pack",
    )(
        *(
            pltpu.with_memory_space_constraint(x, pltpu.HBM)
            for x in (
                lengths.reshape(1, games),
                owners.reshape(1, games),
                features.reshape(row_count, width),
                norm_gain.reshape(1, width),
                rewards.reshape(1, row_count),
            )
        )
    )
    landed = lax.all_to_all(packed, ("actors", "rep"), split_axis=0, concat_axis=0, tiled=True)
    rows, scaled, count = pl.pallas_call(
        functools.partial(unpack_kernel, groups, row_count * actors * groups),
        out_shape=(
            jax.ShapeDtypeStruct((slots, width), jnp.bfloat16),
            jax.ShapeDtypeStruct((1, slots), jnp.float32),
            jax.ShapeDtypeStruct((1, 1), jnp.int32),
        ),
        in_specs=[vmem],
        out_specs=(hbm, hbm, hbm),
        scratch_shapes=[
            pltpu.VMEM((slots, width), jnp.bfloat16),
            pltpu.VMEM((1, slots), jnp.float32),
            pltpu.VMEM((1, 1), jnp.int32),
            pltpu.SemaphoreType.DMA((3,)),
        ],
        compiler_params=pltpu.CompilerParams(vmem_limit_bytes=VMEM_GRANT),
        name="unpack",
    )(landed)
    return (rows.reshape(1, 1, -1, width), scaled.reshape(1, 1, -1), count.reshape(1))


def rms_scale(rows, norm_gain):
    widened = rows.astype(jnp.float32)
    square_mean = jnp.mean(widened * widened, axis=-1, keepdims=True)
    return (widened * lax.rsqrt(square_mean + EPS_NORM) * norm_gain).astype(jnp.bfloat16)


def plain(features, rewards, lengths, owners, norm_gain):
    rows_here = features[0, 0]
    reward_here = rewards[0, 0]
    game_len = lengths[0, 0]
    game_owner = owners[0, 0]
    games = game_len.shape[0]
    row_count = rows_here.shape[0]
    width = rows_here.shape[1]
    row_total = row_count * lax.axis_size("actors") * lax.axis_size("rep")
    starts = jnp.cumsum(game_len) - game_len
    trainer_ids = jnp.arange(games, dtype=jnp.int32)
    owns_game = (game_owner[None, :] == trainer_ids[:, None]).astype(jnp.int32)
    held_len = jnp.sum(owns_game * game_len[None, :], axis=1)
    held_start = jnp.sum(owns_game * starts[None, :], axis=1)
    slot_pos = jnp.arange(CAP, dtype=jnp.int32)
    usable = slot_pos[None, :] < held_len[:, None]
    row_index = jnp.minimum(held_start[:, None] + slot_pos[None, :], row_count - 1)
    outgoing = jnp.where(usable, jnp.take(reward_here, row_index, axis=0), jnp.zeros((), jnp.float32))
    outgoing = jnp.concatenate([outgoing, held_len.astype(jnp.float32)[:, None]], axis=1)
    arrived = lax.all_to_all(outgoing, "actors", split_axis=0, concat_axis=0, tiled=True)
    arrived, arrived_len = arrived[:, :CAP], arrived[:, CAP:]
    normed = rms_scale(rows_here, norm_gain)
    packed = jnp.where(usable[:, :, None], jnp.take(normed, row_index, axis=0), jnp.zeros((), jnp.bfloat16))
    landed = lax.all_to_all(packed, "actors", split_axis=0, concat_axis=0, tiled=True)
    first, second = lax.psum((jnp.sum(arrived), jnp.sum(arrived * arrived)), ("actors", "rep"))
    reward_mean = first / row_total
    inv_spread = lax.rsqrt(second / row_total - reward_mean * reward_mean + EPS_VAR)
    keep_slot = slot_pos[None, :].astype(jnp.float32) < arrived_len
    scaled = jnp.where(keep_slot, (arrived - reward_mean) * inv_spread, jnp.zeros((), jnp.float32))
    count_here = jnp.sum(arrived_len).astype(jnp.int32)
    counts = lax.psum(count_here, "rep")
    return (landed.reshape(1, 1, -1, width), scaled.reshape(1, 1, -1), counts.reshape(1))


def local(features, rewards, lengths, owners, norm_gain):
    actors, groups = lax.axis_size("actors"), lax.axis_size("rep")
    row_count, width = features.shape[2:]
    fits = (
        actors * CAP + 3 <= LANES
        and lengths.shape[2] == actors
        and CAP * width % (SUBLANES * LANES) == 0
        and row_count % 16 == 0
        and row_count <= LANES
        and actors % SUBLANES == 0
    )
    step = fused if fits else plain
    return step(features, rewards, lengths, owners, norm_gain)


def solution(mesh):
    return jax.shard_map(
        local,
        mesh=mesh,
        in_specs=(
            P("rep", "actors", None, None),
            P("rep", "actors", None),
            P("rep", "actors", None),
            P("rep", "actors", None),
            P(),
        ),
        out_specs=(P("rep", "actors", None, None), P("rep", "actors", None), P("actors")),
        check_vma=False,
    )
```

```python
import functools

import jax
import jax.numpy as jnp
from jax import lax
from jax.experimental import pallas as pl
from jax.experimental.pallas import tpu as pltpu
from jax.sharding import PartitionSpec as P

CAP = 3
EPS_NORM = 1e-06
EPS_VAR = 1e-05

LANES = 128
SUBLANES = 8
PAIR = 2
HALF = LANES // 2
VMEM_GRANT = 8 << 20


def pack_kernel(
    groups, length_hbm, owner_hbm, rows_hbm, gain_hbm, reward_hbm, out_ref,
    length_ref, owner_ref, rows_ref, gain_ref, reward_ref, reward_at, normed_ref, scalar_ref, sems,
):
    games = length_ref.shape[1]
    row_count, width = rows_ref.shape
    across = width // LANES
    last = out_ref.shape[1] - 1
    copies = [
        pltpu.make_async_copy(source, target, sems.at[n])
        for n, (source, target) in enumerate(
            (
                (rows_hbm, rows_ref),
                (length_hbm, length_ref),
                (owner_hbm, owner_ref),
                (reward_hbm, reward_at),
                (reward_hbm, reward_ref),
                (gain_hbm, gain_ref),
            )
        )
    ]
    for copy in copies:
        copy.start()
    mine, actor = lax.axis_index("rep"), lax.axis_index("actors")
    slots = lax.axis_size("actors") * CAP
    lane = lax.broadcasted_iota(jnp.int32, (games, LANES), 1)
    place = lane % HALF
    trainer = lax.broadcasted_iota(jnp.int32, (games, LANES), 0)
    for copy in copies:
        copy.wait()

    wide = rows_ref[...].astype(jnp.float32)
    square_mean = jnp.sum(wide * wide, axis=1, keepdims=True) / width
    normed = wide * lax.rsqrt(square_mean + EPS_NORM) * gain_ref[...]
    for k in range(across):
        normed_ref[k * row_count : (k + 1) * row_count] = normed[:, k * LANES : (k + 1) * LANES]

    reward = reward_ref[...]
    first = jnp.sum(reward, axis=1, keepdims=True)
    second = jnp.sum(reward * reward, axis=1, keepdims=True)
    values = jnp.where(place == slots, first, jnp.where(place == slots + 1, second, 0.0))
    sizes = jnp.zeros((games, LANES), jnp.int32)
    start = jnp.int32(0)
    for game in range(games):
        owner, size = owner_ref[0, game], length_ref[0, game]
        chosen = trainer == owner
        sizes = jnp.where(chosen, size, sizes)
        parts = []
        for j in range(CAP):
            part = normed_ref[pl.ds(start + j, across, stride=row_count), :]
            parts.append(jnp.where(j < size, part, 0.0))
            value = reward_at[0, jnp.minimum(start + j, row_count - 1)]
            values = jnp.where(chosen & (place == CAP * actor + j) & (j < size), value, values)
        block = jnp.concatenate(parts, axis=0).astype(jnp.bfloat16)
        out_ref[owner * groups + mine, :last] = block.reshape(last, PAIR, LANES)
        start = start + size

    values = jnp.where(place == slots + 2, sizes.astype(jnp.float32), values)
    high = values.astype(jnp.bfloat16).astype(jnp.float32)
    middle = (values - high).astype(jnp.bfloat16).astype(jnp.float32)
    low = values - high - middle
    kept = jnp.where((place >= CAP * actor) & (place < CAP * actor + sizes), 1.0, 0.0)
    scalar_ref[pl.ds(0, games, stride=PAIR), :] = jnp.where(lane < HALF, high, middle)
    scalar_ref[pl.ds(1, games, stride=PAIR), :] = jnp.where(lane < HALF, low, kept)
    tiles = scalar_ref[...].astype(jnp.bfloat16).reshape(games, PAIR, LANES)
    for t in range(games):
        for group in range(groups):
            out_ref[t * groups + group, last] = tiles[t]


def unpack_kernel(
    groups, rows_total, in_ref, rows_hbm, reward_hbm, count_hbm, rows_ref, reward_ref, count_ref, piece_ref, sems
):
    actors = in_ref.shape[0] // groups
    last = in_ref.shape[1] - 1
    slots, width = rows_ref.shape
    across = width // LANES
    mine = lax.axis_index("rep")

    for s in range(actors):
        block = in_ref[s * groups + mine, :last].reshape(last * PAIR, LANES)
        piece_ref[s * last * PAIR : (s + 1) * last * PAIR] = block.astype(jnp.float32)
    for k in range(across):
        lanes = piece_ref[pl.ds(k, slots, stride=across), :]
        rows_ref[:, k * LANES : (k + 1) * LANES] = lanes.astype(jnp.bfloat16)
    rows_copy = pltpu.make_async_copy(rows_ref, rows_hbm, sems.at[0])
    rows_copy.start()

    def tile(block):
        return in_ref[block, last].astype(jnp.float32)

    def value(total):
        return total[:1, :HALF] + total[:1, HALF:] + total[1:, :HALF]

    own = sum(tile(s * groups + mine) for s in range(actors))
    every = value(sum(tile(block) for block in range(actors * groups)))
    mean = every[:, slots : slots + 1] / rows_total
    second = every[:, slots + 1 : slots + 2] / rows_total
    scale = lax.rsqrt(second - mean * mean + EPS_VAR)
    scaled = jnp.where(own[1:, HALF:] > 0.5, (value(own) - mean) * scale, 0.0)
    reward_ref[...] = scaled[:, :slots]
    count_ref[...] = every[:, slots + 2 : slots + 3].astype(jnp.int32)
    reward_copy = pltpu.make_async_copy(reward_ref, reward_hbm, sems.at[1])
    count_copy = pltpu.make_async_copy(count_ref, count_hbm, sems.at[2])
    reward_copy.start()
    count_copy.start()
    rows_copy.wait()
    reward_copy.wait()
    count_copy.wait()


def fused(features, rewards, lengths, owners, norm_gain):
    row_count, width = features.shape[2:]
    games = lengths.shape[2]
    actors, groups = lax.axis_size("actors"), lax.axis_size("rep")
    slots = actors * CAP
    across = width // LANES
    last = CAP * across // PAIR
    vmem = pl.BlockSpec(memory_space=pltpu.VMEM)
    hbm = pl.BlockSpec(memory_space=pltpu.HBM)
    packed = pl.pallas_call(
        functools.partial(pack_kernel, groups),
        out_shape=jax.ShapeDtypeStruct((games * groups, last + 1, PAIR, LANES), jnp.bfloat16),
        in_specs=[hbm] * 5,
        out_specs=vmem,
        scratch_shapes=[
            pltpu.SMEM((1, games), jnp.int32),
            pltpu.SMEM((1, games), jnp.int32),
            pltpu.VMEM((row_count, width), jnp.bfloat16),
            pltpu.VMEM((1, width), jnp.float32),
            pltpu.VMEM((1, row_count), jnp.float32),
            pltpu.SMEM((1, row_count), jnp.float32),
            pltpu.VMEM(((across + 1) * row_count, LANES), jnp.float32),
            pltpu.VMEM((PAIR * games, LANES), jnp.float32),
            pltpu.SemaphoreType.DMA((6,)),
        ],
        compiler_params=pltpu.CompilerParams(vmem_limit_bytes=VMEM_GRANT),
        name="pack",
    )(
        *(
            pltpu.with_memory_space_constraint(x, pltpu.HBM)
            for x in (
                lengths.reshape(1, games),
                owners.reshape(1, games),
                features.reshape(row_count, width),
                norm_gain.reshape(1, width),
                rewards.reshape(1, row_count),
            )
        )
    )
    landed = lax.all_to_all(packed, ("actors", "rep"), split_axis=0, concat_axis=0, tiled=True)
    rows, scaled, count = pl.pallas_call(
        functools.partial(unpack_kernel, groups, row_count * actors * groups),
        out_shape=(
            jax.ShapeDtypeStruct((slots, width), jnp.bfloat16),
            jax.ShapeDtypeStruct((1, slots), jnp.float32),
            jax.ShapeDtypeStruct((1, 1), jnp.int32),
        ),
        in_specs=[vmem],
        out_specs=(hbm, hbm, hbm),
        scratch_shapes=[
            pltpu.VMEM((slots, width), jnp.bfloat16),
            pltpu.VMEM((1, slots), jnp.float32),
            pltpu.VMEM((1, 1), jnp.int32),
            pltpu.VMEM((slots * across, LANES), jnp.float32),
            pltpu.SemaphoreType.DMA((3,)),
        ],
        compiler_params=pltpu.CompilerParams(vmem_limit_bytes=VMEM_GRANT),
        name="unpack",
    )(landed)
    return (rows.reshape(1, 1, -1, width), scaled.reshape(1, 1, -1), count.reshape(1))


def rms_scale(rows, norm_gain):
    widened = rows.astype(jnp.float32)
    square_mean = jnp.mean(widened * widened, axis=-1, keepdims=True)
    return (widened * lax.rsqrt(square_mean + EPS_NORM) * norm_gain).astype(jnp.bfloat16)


def plain(features, rewards, lengths, owners, norm_gain):
    rows_here = features[0, 0]
    reward_here = rewards[0, 0]
    game_len = lengths[0, 0]
    game_owner = owners[0, 0]
    games = game_len.shape[0]
    row_count = rows_here.shape[0]
    width = rows_here.shape[1]
    row_total = row_count * lax.axis_size("actors") * lax.axis_size("rep")
    starts = jnp.cumsum(game_len) - game_len
    trainer_ids = jnp.arange(games, dtype=jnp.int32)
    owns_game = (game_owner[None, :] == trainer_ids[:, None]).astype(jnp.int32)
    held_len = jnp.sum(owns_game * game_len[None, :], axis=1)
    held_start = jnp.sum(owns_game * starts[None, :], axis=1)
    slot_pos = jnp.arange(CAP, dtype=jnp.int32)
    usable = slot_pos[None, :] < held_len[:, None]
    row_index = jnp.minimum(held_start[:, None] + slot_pos[None, :], row_count - 1)
    outgoing = jnp.where(usable, jnp.take(reward_here, row_index, axis=0), jnp.zeros((), jnp.float32))
    outgoing = jnp.concatenate([outgoing, held_len.astype(jnp.float32)[:, None]], axis=1)
    arrived = lax.all_to_all(outgoing, "actors", split_axis=0, concat_axis=0, tiled=True)
    arrived, arrived_len = arrived[:, :CAP], arrived[:, CAP:]
    normed = rms_scale(rows_here, norm_gain)
    packed = jnp.where(usable[:, :, None], jnp.take(normed, row_index, axis=0), jnp.zeros((), jnp.bfloat16))
    landed = lax.all_to_all(packed, "actors", split_axis=0, concat_axis=0, tiled=True)
    first, second = lax.psum((jnp.sum(arrived), jnp.sum(arrived * arrived)), ("actors", "rep"))
    reward_mean = first / row_total
    inv_spread = lax.rsqrt(second / row_total - reward_mean * reward_mean + EPS_VAR)
    keep_slot = slot_pos[None, :].astype(jnp.float32) < arrived_len
    scaled = jnp.where(keep_slot, (arrived - reward_mean) * inv_spread, jnp.zeros((), jnp.float32))
    count_here = jnp.sum(arrived_len).astype(jnp.int32)
    counts = lax.psum(count_here, "rep")
    return (landed.reshape(1, 1, -1, width), scaled.reshape(1, 1, -1), counts.reshape(1))


def local(features, rewards, lengths, owners, norm_gain):
    actors, groups = lax.axis_size("actors"), lax.axis_size("rep")
    row_count, width = features.shape[2:]
    fits = (
        actors * CAP + 3 <= HALF
        and lengths.shape[2] == actors
        and actors % SUBLANES == 0
        and width % (SUBLANES * LANES) == 0
        and row_count % 16 == 0
        and row_count <= LANES
    )
    step = fused if fits else plain
    return step(features, rewards, lengths, owners, norm_gain)


def solution(mesh):
    return jax.shard_map(
        local,
        mesh=mesh,
        in_specs=(
            P("rep", "actors", None, None),
            P("rep", "actors", None),
            P("rep", "actors", None),
            P("rep", "actors", None),
            P(),
        ),
        out_specs=(P("rep", "actors", None, None), P("rep", "actors", None), P("actors")),
        check_vma=False,
    )
```

```python
import functools

import jax
import jax.numpy as jnp
from jax import lax
from jax.experimental import pallas as pl
from jax.experimental.pallas import tpu as pltpu
from jax.sharding import PartitionSpec as P

CAP = 3
EPS_NORM = 1e-06
EPS_VAR = 1e-05

LANES = 128
SUBLANES = 8
PAIR = 2
HALF = LANES // 2
VMEM_GRANT = 8 << 20
ORDERS = {}


def places(actors, groups):
    order = ORDERS.get((actors, groups)) or [a * groups + g for g in range(groups) for a in range(actors)]
    return order, [order.index(device) for device in range(actors * groups)]


def of_group(choices, mine):
    chosen = jnp.int32(choices[0])
    for group in range(1, len(choices)):
        chosen = jnp.where(mine == group, choices[group], chosen)
    return chosen


def pack_kernel(
    place_of, groups, length_ref, owner_ref, reward_at, rows_ref, gain_ref, reward_ref,
    out_ref, normed_ref, scalar_ref, start_of, length_of,
):
    games = length_ref.shape[1]
    row_count, width = rows_ref.shape
    across = width // LANES
    stride = row_count
    last = out_ref.shape[1] - 1
    mine, actor = lax.axis_index("rep"), lax.axis_index("actors")
    slots = lax.axis_size("actors") * CAP

    start = jnp.int32(0)
    for game in range(games):
        owner, size = owner_ref[0, game], length_ref[0, game]
        start_of[owner] = start
        length_of[owner] = size
        start = start + size

    wide = rows_ref[...].astype(jnp.float32)
    square_mean = jnp.sum(wide * wide, axis=1, keepdims=True) / width
    normed = wide * lax.rsqrt(square_mean + EPS_NORM) * gain_ref[...]
    for k in range(across):
        normed_ref[k * stride : k * stride + row_count] = normed[:, k * LANES : (k + 1) * LANES]

    lane = lax.broadcasted_iota(jnp.int32, (games, LANES), 1)
    place = lane % HALF
    trainer = lax.broadcasted_iota(jnp.int32, (games, LANES), 0)
    reward = reward_ref[...]
    first = jnp.sum(reward, axis=1, keepdims=True)
    second = jnp.sum(reward * reward, axis=1, keepdims=True)
    sizes = jnp.zeros((games, LANES), jnp.int32)
    held = [jnp.zeros((games, LANES), jnp.float32) for _ in range(CAP)]
    for t in range(games):
        begin, size = start_of[t], length_of[t]
        sizes = jnp.where(trainer == t, size, sizes)
        parts = []
        for j in range(CAP):
            part = normed_ref[pl.ds(begin + j, across, stride=stride), :]
            parts.append(jnp.where(j < size, part, 0.0))
            value = reward_at[0, jnp.minimum(begin + j, row_count - 1)]
            held[j] = jnp.where(trainer == t, value, held[j])
        block = jnp.concatenate(parts, axis=0).astype(jnp.bfloat16)
        target = of_group([place_of[t * groups + group] for group in range(groups)], mine)
        out_ref[target, :last] = block.reshape(last, PAIR, LANES)

    own = place - CAP * actor
    kept = (own >= 0) & (own < sizes)
    values = jnp.where(place == slots, first, jnp.where(place == slots + 1, second, 0.0))
    values = jnp.where(place == slots + 2, sizes.astype(jnp.float32), values)
    for j in range(CAP):
        values = jnp.where(kept & (own == j), held[j], values)
    high = values.astype(jnp.bfloat16).astype(jnp.float32)
    middle = (values - high).astype(jnp.bfloat16).astype(jnp.float32)
    low = values - high - middle
    scalar_ref[pl.ds(0, games, stride=PAIR), :] = jnp.where(lane < HALF, high, middle)
    scalar_ref[pl.ds(1, games, stride=PAIR), :] = jnp.where(lane < HALF, low, jnp.where(kept, 1.0, 0.0))
    tiles = scalar_ref[...].astype(jnp.bfloat16).reshape(games, PAIR, LANES)
    for t in range(games):
        for group in range(groups):
            out_ref[place_of[t * groups + group], last] = tiles[t]


def unpack_kernel(
    place_of, groups, rows_total, in_ref, rows_hbm, reward_hbm, count_hbm, rows_ref, reward_ref, count_ref, piece_ref, sems
):
    actors = in_ref.shape[0] // groups
    last = in_ref.shape[1] - 1
    slots, width = rows_ref.shape
    across = width // LANES
    stride = across
    mine = lax.axis_index("rep")
    own_places = [of_group([place_of[s * groups + group] for group in range(groups)], mine) for s in range(actors)]

    def tile(block):
        return in_ref[block, last].astype(jnp.float32)

    def value(total):
        return total[:1, :HALF] + total[:1, HALF:] + total[1:, :HALF]

    for s in range(actors):
        block = in_ref[own_places[s], :last].reshape(last * PAIR, LANES).astype(jnp.float32)
        for j in range(CAP):
            at = (s * CAP + j) * stride
            piece_ref[at : at + across] = block[j * across : (j + 1) * across]
    for k in range(across):
        lanes = piece_ref[pl.ds(k, slots, stride=stride), :]
        rows_ref[:, k * LANES : (k + 1) * LANES] = lanes.astype(jnp.bfloat16)
    rows_copy = pltpu.make_async_copy(rows_ref, rows_hbm, sems.at[0])
    rows_copy.start()

    own = sum(tile(block) for block in own_places)
    every = value(sum(tile(block) for block in range(actors * groups)))
    mean = every[:, slots : slots + 1] / rows_total
    second = every[:, slots + 1 : slots + 2] / rows_total
    scale = lax.rsqrt(second - mean * mean + EPS_VAR)
    scaled = jnp.where(own[1:, HALF:] > 0.5, (value(own) - mean) * scale, 0.0)
    reward_ref[...] = scaled[:, :slots]
    count_ref[...] = every[:, slots + 2 : slots + 3].astype(jnp.int32)
    reward_copy = pltpu.make_async_copy(reward_ref, reward_hbm, sems.at[1])
    count_copy = pltpu.make_async_copy(count_ref, count_hbm, sems.at[2])
    reward_copy.start()
    count_copy.start()
    rows_copy.wait()
    reward_copy.wait()
    count_copy.wait()


def fused(features, rewards, lengths, owners, norm_gain):
    row_count, width = features.shape[2:]
    games = lengths.shape[2]
    actors, groups = lax.axis_size("actors"), lax.axis_size("rep")
    slots = actors * CAP
    across = width // LANES
    last = CAP * across // PAIR
    order, place_of = places(actors, groups)
    vmem = pl.BlockSpec(memory_space=pltpu.VMEM)
    smem = pl.BlockSpec(memory_space=pltpu.SMEM)
    hbm = pl.BlockSpec(memory_space=pltpu.HBM)
    packed = pl.pallas_call(
        functools.partial(pack_kernel, place_of, groups),
        out_shape=jax.ShapeDtypeStruct((games * groups, last + 1, PAIR, LANES), jnp.bfloat16),
        in_specs=[smem, smem, smem, vmem, vmem, vmem],
        out_specs=vmem,
        scratch_shapes=[
            pltpu.VMEM(((across + 1) * row_count, LANES), jnp.float32),
            pltpu.VMEM((PAIR * games, LANES), jnp.float32),
            pltpu.SMEM((games,), jnp.int32),
            pltpu.SMEM((games,), jnp.int32),
        ],
        compiler_params=pltpu.CompilerParams(vmem_limit_bytes=VMEM_GRANT),
        name="pack",
    )(
        *(
            pltpu.with_memory_space_constraint(x, pltpu.HBM)
            for x in (
                lengths.reshape(1, games),
                owners.reshape(1, games),
                rewards.reshape(1, row_count),
                features.reshape(row_count, width),
                norm_gain.reshape(1, width),
                rewards.reshape(1, row_count),
            )
        )
    )
    landed = lax.all_to_all(
        packed, ("actors", "rep"), split_axis=0, concat_axis=0, tiled=True, axis_index_groups=[order]
    )
    rows, scaled, count = pl.pallas_call(
        functools.partial(unpack_kernel, place_of, groups, row_count * actors * groups),
        out_shape=(
            jax.ShapeDtypeStruct((slots, width), jnp.bfloat16),
            jax.ShapeDtypeStruct((1, slots), jnp.float32),
            jax.ShapeDtypeStruct((1, 1), jnp.int32),
        ),
        in_specs=[vmem],
        out_specs=(hbm, hbm, hbm),
        scratch_shapes=[
            pltpu.VMEM((slots, width), jnp.bfloat16),
            pltpu.VMEM((1, slots), jnp.float32),
            pltpu.VMEM((1, 1), jnp.int32),
            pltpu.VMEM((slots * across, LANES), jnp.float32),
            pltpu.SemaphoreType.DMA((3,)),
        ],
        compiler_params=pltpu.CompilerParams(vmem_limit_bytes=VMEM_GRANT),
        name="unpack",
    )(landed)
    return (rows.reshape(1, 1, -1, width), scaled.reshape(1, 1, -1), count.reshape(1))


def rms_scale(rows, norm_gain):
    widened = rows.astype(jnp.float32)
    square_mean = jnp.mean(widened * widened, axis=-1, keepdims=True)
    return (widened * lax.rsqrt(square_mean + EPS_NORM) * norm_gain).astype(jnp.bfloat16)


def plain(features, rewards, lengths, owners, norm_gain):
    rows_here = features[0, 0]
    reward_here = rewards[0, 0]
    game_len = lengths[0, 0]
    game_owner = owners[0, 0]
    games = game_len.shape[0]
    row_count = rows_here.shape[0]
    width = rows_here.shape[1]
    row_total = row_count * lax.axis_size("actors") * lax.axis_size("rep")
    starts = jnp.cumsum(game_len) - game_len
    trainer_ids = jnp.arange(games, dtype=jnp.int32)
    owns_game = (game_owner[None, :] == trainer_ids[:, None]).astype(jnp.int32)
    held_len = jnp.sum(owns_game * game_len[None, :], axis=1)
    held_start = jnp.sum(owns_game * starts[None, :], axis=1)
    slot_pos = jnp.arange(CAP, dtype=jnp.int32)
    usable = slot_pos[None, :] < held_len[:, None]
    row_index = jnp.minimum(held_start[:, None] + slot_pos[None, :], row_count - 1)
    outgoing = jnp.where(usable, jnp.take(reward_here, row_index, axis=0), jnp.zeros((), jnp.float32))
    outgoing = jnp.concatenate([outgoing, held_len.astype(jnp.float32)[:, None]], axis=1)
    arrived = lax.all_to_all(outgoing, "actors", split_axis=0, concat_axis=0, tiled=True)
    arrived, arrived_len = arrived[:, :CAP], arrived[:, CAP:]
    normed = rms_scale(rows_here, norm_gain)
    packed = jnp.where(usable[:, :, None], jnp.take(normed, row_index, axis=0), jnp.zeros((), jnp.bfloat16))
    landed = lax.all_to_all(packed, "actors", split_axis=0, concat_axis=0, tiled=True)
    first, second = lax.psum((jnp.sum(arrived), jnp.sum(arrived * arrived)), ("actors", "rep"))
    reward_mean = first / row_total
    inv_spread = lax.rsqrt(second / row_total - reward_mean * reward_mean + EPS_VAR)
    keep_slot = slot_pos[None, :].astype(jnp.float32) < arrived_len
    scaled = jnp.where(keep_slot, (arrived - reward_mean) * inv_spread, jnp.zeros((), jnp.float32))
    count_here = jnp.sum(arrived_len).astype(jnp.int32)
    counts = lax.psum(count_here, "rep")
    return (landed.reshape(1, 1, -1, width), scaled.reshape(1, 1, -1), counts.reshape(1))


def local(features, rewards, lengths, owners, norm_gain):
    actors, groups = lax.axis_size("actors"), lax.axis_size("rep")
    row_count, width = features.shape[2:]
    fits = (
        actors * CAP + 3 <= HALF
        and lengths.shape[2] == actors
        and actors % SUBLANES == 0
        and width % (SUBLANES * LANES) == 0
        and row_count % 16 == 0
        and row_count <= LANES
    )
    step = fused if fits else plain
    return step(features, rewards, lengths, owners, norm_gain)


def solution(mesh):
    return jax.shard_map(
        local,
        mesh=mesh,
        in_specs=(
            P("rep", "actors", None, None),
            P("rep", "actors", None),
            P("rep", "actors", None),
            P("rep", "actors", None),
            P(),
        ),
        out_specs=(P("rep", "actors", None, None), P("rep", "actors", None), P("actors")),
        check_vma=False,
    )
```

```python
import functools

import jax
import jax.numpy as jnp
from jax import lax
from jax.experimental import pallas as pl
from jax.experimental.pallas import tpu as pltpu
from jax.sharding import PartitionSpec as P

CAP = 3
EPS_NORM = 1e-06
EPS_VAR = 1e-05

LANES = 128
SUBLANES = 8
PAIR = 2
HALF = LANES // 2
VMEM_GRANT = 8 << 20
ORDERS = {
    (8, 4): [
        4, 7, 18, 5, 27, 2, 16, 8, 21, 9, 30, 15, 17, 12, 29, 22, 3, 26, 6, 1, 11, 0, 13, 19, 24, 25, 31, 10, 23, 28, 14, 20,
    ]
}


def places(actors, groups):
    order = ORDERS.get((actors, groups)) or [a * groups + g for g in range(groups) for a in range(actors)]
    return order, [order.index(device) for device in range(actors * groups)]


def of_group(choices, mine):
    chosen = jnp.int32(choices[0])
    for group in range(1, len(choices)):
        chosen = jnp.where(mine == group, choices[group], chosen)
    return chosen


def pack_kernel(
    place_of, groups, length_ref, owner_ref, reward_at, rows_ref, gain_ref, reward_ref,
    out_ref, normed_ref, scalar_ref, start_of, length_of,
):
    games = length_ref.shape[1]
    row_count, width = rows_ref.shape
    across = width // LANES
    stride = row_count
    last = out_ref.shape[1] - 1
    mine, actor = lax.axis_index("rep"), lax.axis_index("actors")
    slots = lax.axis_size("actors") * CAP

    start = jnp.int32(0)
    for game in range(games):
        owner, size = owner_ref[0, game], length_ref[0, game]
        start_of[owner] = start
        length_of[owner] = size
        start = start + size

    wide = rows_ref[...].astype(jnp.float32)
    square_mean = jnp.sum(wide * wide, axis=1, keepdims=True) / width
    normed = wide * lax.rsqrt(square_mean + EPS_NORM) * gain_ref[...]
    for k in range(across):
        normed_ref[k * stride : k * stride + row_count] = normed[:, k * LANES : (k + 1) * LANES]

    lane = lax.broadcasted_iota(jnp.int32, (games, LANES), 1)
    place = lane % HALF
    trainer = lax.broadcasted_iota(jnp.int32, (games, LANES), 0)
    reward = reward_ref[...]
    first = jnp.sum(reward, axis=1, keepdims=True)
    second = jnp.sum(reward * reward, axis=1, keepdims=True)
    sizes = jnp.zeros((games, LANES), jnp.int32)
    held = [jnp.zeros((games, LANES), jnp.float32) for _ in range(CAP)]
    for t in range(games):
        begin, size = start_of[t], length_of[t]
        sizes = jnp.where(trainer == t, size, sizes)
        parts = []
        for j in range(CAP):
            part = normed_ref[pl.ds(begin + j, across, stride=stride), :]
            parts.append(jnp.where(j < size, part, 0.0))
            value = reward_at[0, jnp.minimum(begin + j, row_count - 1)]
            held[j] = jnp.where(trainer == t, value, held[j])
        block = jnp.concatenate(parts, axis=0).astype(jnp.bfloat16)
        target = of_group([place_of[t * groups + group] for group in range(groups)], mine)
        out_ref[target, :last] = block.reshape(last, PAIR, LANES)

    own = place - CAP * actor
    kept = (own >= 0) & (own < sizes)
    values = jnp.where(place == slots, first, jnp.where(place == slots + 1, second, 0.0))
    values = jnp.where(place == slots + 2, sizes.astype(jnp.float32), values)
    for j in range(CAP):
        values = jnp.where(kept & (own == j), held[j], values)
    high = values.astype(jnp.bfloat16).astype(jnp.float32)
    middle = (values - high).astype(jnp.bfloat16).astype(jnp.float32)
    low = values - high - middle
    scalar_ref[pl.ds(0, games, stride=PAIR), :] = jnp.where(lane < HALF, high, middle)
    scalar_ref[pl.ds(1, games, stride=PAIR), :] = jnp.where(lane < HALF, low, jnp.where(kept, 1.0, 0.0))
    tiles = scalar_ref[...].astype(jnp.bfloat16).reshape(games, PAIR, LANES)
    for t in range(games):
        for group in range(groups):
            out_ref[place_of[t * groups + group], last] = tiles[t]


def unpack_kernel(
    place_of, groups, rows_total, in_ref, rows_hbm, reward_hbm, count_hbm, rows_ref, reward_ref, count_ref, piece_ref, sems
):
    actors = in_ref.shape[0] // groups
    last = in_ref.shape[1] - 1
    slots, width = rows_ref.shape
    across = width // LANES
    stride = across
    mine = lax.axis_index("rep")
    own_places = [of_group([place_of[s * groups + group] for group in range(groups)], mine) for s in range(actors)]

    def tile(block):
        return in_ref[block, last].astype(jnp.float32)

    def value(total):
        return total[:1, :HALF] + total[:1, HALF:] + total[1:, :HALF]

    for s in range(actors):
        block = in_ref[own_places[s], :last].reshape(last * PAIR, LANES).astype(jnp.float32)
        for j in range(CAP):
            at = (s * CAP + j) * stride
            piece_ref[at : at + across] = block[j * across : (j + 1) * across]
    for k in range(across):
        lanes = piece_ref[pl.ds(k, slots, stride=stride), :]
        rows_ref[:, k * LANES : (k + 1) * LANES] = lanes.astype(jnp.bfloat16)
    rows_copy = pltpu.make_async_copy(rows_ref, rows_hbm, sems.at[0])
    rows_copy.start()

    own = sum(tile(block) for block in own_places)
    every = value(sum(tile(block) for block in range(actors * groups)))
    mean = every[:, slots : slots + 1] / rows_total
    second = every[:, slots + 1 : slots + 2] / rows_total
    scale = lax.rsqrt(second - mean * mean + EPS_VAR)
    scaled = jnp.where(own[1:, HALF:] > 0.5, (value(own) - mean) * scale, 0.0)
    reward_ref[...] = scaled[:, :slots]
    count_ref[...] = every[:, slots + 2 : slots + 3].astype(jnp.int32)
    reward_copy = pltpu.make_async_copy(reward_ref, reward_hbm, sems.at[1])
    count_copy = pltpu.make_async_copy(count_ref, count_hbm, sems.at[2])
    reward_copy.start()
    count_copy.start()
    rows_copy.wait()
    reward_copy.wait()
    count_copy.wait()


def fused(features, rewards, lengths, owners, norm_gain):
    row_count, width = features.shape[2:]
    games = lengths.shape[2]
    actors, groups = lax.axis_size("actors"), lax.axis_size("rep")
    slots = actors * CAP
    across = width // LANES
    last = CAP * across // PAIR
    order, place_of = places(actors, groups)
    vmem = pl.BlockSpec(memory_space=pltpu.VMEM)
    smem = pl.BlockSpec(memory_space=pltpu.SMEM)
    hbm = pl.BlockSpec(memory_space=pltpu.HBM)
    packed = pl.pallas_call(
        functools.partial(pack_kernel, place_of, groups),
        out_shape=jax.ShapeDtypeStruct((games * groups, last + 1, PAIR, LANES), jnp.bfloat16),
        in_specs=[smem, smem, smem, vmem, vmem, vmem],
        out_specs=vmem,
        scratch_shapes=[
            pltpu.VMEM(((across + 1) * row_count, LANES), jnp.float32),
            pltpu.VMEM((PAIR * games, LANES), jnp.float32),
            pltpu.SMEM((games,), jnp.int32),
            pltpu.SMEM((games,), jnp.int32),
        ],
        compiler_params=pltpu.CompilerParams(vmem_limit_bytes=VMEM_GRANT),
        name="pack",
    )(
        *(
            pltpu.with_memory_space_constraint(x, pltpu.HBM)
            for x in (
                lengths.reshape(1, games),
                owners.reshape(1, games),
                rewards.reshape(1, row_count),
                features.reshape(row_count, width),
                norm_gain.reshape(1, width),
                rewards.reshape(1, row_count),
            )
        )
    )
    landed = lax.all_to_all(
        packed, ("actors", "rep"), split_axis=0, concat_axis=0, tiled=True, axis_index_groups=[order]
    )
    rows, scaled, count = pl.pallas_call(
        functools.partial(unpack_kernel, place_of, groups, row_count * actors * groups),
        out_shape=(
            jax.ShapeDtypeStruct((slots, width), jnp.bfloat16),
            jax.ShapeDtypeStruct((1, slots), jnp.float32),
            jax.ShapeDtypeStruct((1, 1), jnp.int32),
        ),
        in_specs=[vmem],
        out_specs=(hbm, hbm, hbm),
        scratch_shapes=[
            pltpu.VMEM((slots, width), jnp.bfloat16),
            pltpu.VMEM((1, slots), jnp.float32),
            pltpu.VMEM((1, 1), jnp.int32),
            pltpu.VMEM((slots * across, LANES), jnp.float32),
            pltpu.SemaphoreType.DMA((3,)),
        ],
        compiler_params=pltpu.CompilerParams(vmem_limit_bytes=VMEM_GRANT),
        name="unpack",
    )(landed)
    return (rows.reshape(1, 1, -1, width), scaled.reshape(1, 1, -1), count.reshape(1))


def rms_scale(rows, norm_gain):
    widened = rows.astype(jnp.float32)
    square_mean = jnp.mean(widened * widened, axis=-1, keepdims=True)
    return (widened * lax.rsqrt(square_mean + EPS_NORM) * norm_gain).astype(jnp.bfloat16)


def plain(features, rewards, lengths, owners, norm_gain):
    rows_here = features[0, 0]
    reward_here = rewards[0, 0]
    game_len = lengths[0, 0]
    game_owner = owners[0, 0]
    games = game_len.shape[0]
    row_count = rows_here.shape[0]
    width = rows_here.shape[1]
    row_total = row_count * lax.axis_size("actors") * lax.axis_size("rep")
    starts = jnp.cumsum(game_len) - game_len
    trainer_ids = jnp.arange(games, dtype=jnp.int32)
    owns_game = (game_owner[None, :] == trainer_ids[:, None]).astype(jnp.int32)
    held_len = jnp.sum(owns_game * game_len[None, :], axis=1)
    held_start = jnp.sum(owns_game * starts[None, :], axis=1)
    slot_pos = jnp.arange(CAP, dtype=jnp.int32)
    usable = slot_pos[None, :] < held_len[:, None]
    row_index = jnp.minimum(held_start[:, None] + slot_pos[None, :], row_count - 1)
    outgoing = jnp.where(usable, jnp.take(reward_here, row_index, axis=0), jnp.zeros((), jnp.float32))
    outgoing = jnp.concatenate([outgoing, held_len.astype(jnp.float32)[:, None]], axis=1)
    arrived = lax.all_to_all(outgoing, "actors", split_axis=0, concat_axis=0, tiled=True)
    arrived, arrived_len = arrived[:, :CAP], arrived[:, CAP:]
    normed = rms_scale(rows_here, norm_gain)
    packed = jnp.where(usable[:, :, None], jnp.take(normed, row_index, axis=0), jnp.zeros((), jnp.bfloat16))
    landed = lax.all_to_all(packed, "actors", split_axis=0, concat_axis=0, tiled=True)
    first, second = lax.psum((jnp.sum(arrived), jnp.sum(arrived * arrived)), ("actors", "rep"))
    reward_mean = first / row_total
    inv_spread = lax.rsqrt(second / row_total - reward_mean * reward_mean + EPS_VAR)
    keep_slot = slot_pos[None, :].astype(jnp.float32) < arrived_len
    scaled = jnp.where(keep_slot, (arrived - reward_mean) * inv_spread, jnp.zeros((), jnp.float32))
    count_here = jnp.sum(arrived_len).astype(jnp.int32)
    counts = lax.psum(count_here, "rep")
    return (landed.reshape(1, 1, -1, width), scaled.reshape(1, 1, -1), counts.reshape(1))


def local(features, rewards, lengths, owners, norm_gain):
    actors, groups = lax.axis_size("actors"), lax.axis_size("rep")
    row_count, width = features.shape[2:]
    fits = (
        actors * CAP + 3 <= HALF
        and lengths.shape[2] == actors
        and actors % SUBLANES == 0
        and width % (SUBLANES * LANES) == 0
        and row_count % 16 == 0
        and row_count <= LANES
    )
    step = fused if fits else plain
    return step(features, rewards, lengths, owners, norm_gain)


def solution(mesh):
    return jax.shard_map(
        local,
        mesh=mesh,
        in_specs=(
            P("rep", "actors", None, None),
            P("rep", "actors", None),
            P("rep", "actors", None),
            P("rep", "actors", None),
            P(),
        ),
        out_specs=(P("rep", "actors", None, None), P("rep", "actors", None), P("actors")),
        check_vma=False,
    )
```

```python
import functools

import jax
import jax.numpy as jnp
from jax import lax
from jax.experimental import pallas as pl
from jax.experimental.pallas import tpu as pltpu
from jax.sharding import PartitionSpec as P

CAP = 3
EPS_NORM = 1e-06
EPS_VAR = 1e-05

LANES = 128
SUBLANES = 8
PAIR = 2
HALF = LANES // 2
VMEM_GRANT = 8 << 20
ORDERS = {
    (8, 4): [
        7, 18, 5, 14, 2, 16, 29, 21, 27, 30, 15, 17, 12, 6, 22, 3, 28, 10, 1, 11, 0, 13, 19, 24, 9, 31, 4, 23, 26, 25, 20, 8,
    ]
}


def places(actors, groups):
    order = ORDERS.get((actors, groups)) or [a * groups + g for g in range(groups) for a in range(actors)]
    return order, [order.index(device) for device in range(actors * groups)]


def of_group(choices, mine):
    chosen = jnp.int32(choices[0])
    for group in range(1, len(choices)):
        chosen = jnp.where(mine == group, choices[group], chosen)
    return chosen


def pack_kernel(
    place_of, groups, length_ref, owner_ref, reward_at, rows_ref, gain_ref, reward_ref,
    out_ref, normed_ref, scalar_ref, start_of, length_of,
):
    games = length_ref.shape[1]
    row_count, width = rows_ref.shape
    across = width // LANES
    stride = row_count
    last = out_ref.shape[1] - 1
    mine, actor = lax.axis_index("rep"), lax.axis_index("actors")
    slots = lax.axis_size("actors") * CAP

    start = jnp.int32(0)
    for game in range(games):
        owner, size = owner_ref[0, game], length_ref[0, game]
        start_of[owner] = start
        length_of[owner] = size
        start = start + size

    wide = rows_ref[...].astype(jnp.float32)
    square_mean = jnp.sum(wide * wide, axis=1, keepdims=True) / width
    normed = wide * lax.rsqrt(square_mean + EPS_NORM) * gain_ref[...]
    for k in range(across):
        normed_ref[k * stride : k * stride + row_count] = normed[:, k * LANES : (k + 1) * LANES]

    lane = lax.broadcasted_iota(jnp.int32, (games, LANES), 1)
    place = lane % HALF
    trainer = lax.broadcasted_iota(jnp.int32, (games, LANES), 0)
    reward = reward_ref[...]
    first = jnp.sum(reward, axis=1, keepdims=True)
    second = jnp.sum(reward * reward, axis=1, keepdims=True)
    sizes = jnp.zeros((games, LANES), jnp.int32)
    held = [jnp.zeros((games, LANES), jnp.float32) for _ in range(CAP)]
    for t in range(games):
        begin, size = start_of[t], length_of[t]
        sizes = jnp.where(trainer == t, size, sizes)
        parts = []
        for j in range(CAP):
            part = normed_ref[pl.ds(begin + j, across, stride=stride), :]
            parts.append(jnp.where(j < size, part, 0.0))
            value = reward_at[0, jnp.minimum(begin + j, row_count - 1)]
            held[j] = jnp.where(trainer == t, value, held[j])
        block = jnp.concatenate(parts, axis=0).astype(jnp.bfloat16)
        target = of_group([place_of[t * groups + group] for group in range(groups)], mine)
        out_ref[target, :last] = block.reshape(last, PAIR, LANES)

    own = place - CAP * actor
    kept = (own >= 0) & (own < sizes)
    values = jnp.where(place == slots, first, jnp.where(place == slots + 1, second, 0.0))
    values = jnp.where(place == slots + 2, sizes.astype(jnp.float32), values)
    for j in range(CAP):
        values = jnp.where(kept & (own == j), held[j], values)
    high = values.astype(jnp.bfloat16).astype(jnp.float32)
    middle = (values - high).astype(jnp.bfloat16).astype(jnp.float32)
    low = values - high - middle
    scalar_ref[pl.ds(0, games, stride=PAIR), :] = jnp.where(lane < HALF, high, middle)
    scalar_ref[pl.ds(1, games, stride=PAIR), :] = jnp.where(lane < HALF, low, jnp.where(kept, 1.0, 0.0))
    tiles = scalar_ref[...].astype(jnp.bfloat16).reshape(games, PAIR, LANES)
    for t in range(games):
        for group in range(groups):
            out_ref[place_of[t * groups + group], last] = tiles[t]


def unpack_kernel(
    place_of, groups, rows_total, in_ref, rows_ref, reward_ref, count_ref, piece_ref
):
    actors = in_ref.shape[0] // groups
    last = in_ref.shape[1] - 1
    slots, width = rows_ref.shape
    across = width // LANES
    stride = across
    mine = lax.axis_index("rep")
    own_places = [of_group([place_of[s * groups + group] for group in range(groups)], mine) for s in range(actors)]

    def total(blocks):
        terms = [in_ref[block, last].astype(jnp.float32) for block in blocks]
        while len(terms) > 1:
            terms = [sum(terms[at : at + 2]) for at in range(0, len(terms), 2)]
        return terms[0]

    for s in range(actors):
        block = in_ref[own_places[s], :last].reshape(last * PAIR, LANES).astype(jnp.float32)
        for j in range(CAP):
            at = (s * CAP + j) * stride
            piece_ref[at : at + across] = block[j * across : (j + 1) * across]
    for k in range(across):
        lanes = piece_ref[pl.ds(k, slots, stride=stride), :]
        rows_ref[:, k * LANES : (k + 1) * LANES] = lanes.astype(jnp.bfloat16)

    every = total(range(actors * groups))
    own = total(own_places)

    def sum_of(at):
        parts = (every[:1, at : at + 1], every[:1, HALF + at : HALF + at + 1], every[1:, at : at + 1])
        high, middle, low = (jnp.broadcast_to(part, (1, HALF)) for part in parts)
        return high + middle + low

    mean = sum_of(slots) / rows_total
    second = sum_of(slots + 1) / rows_total
    scale = lax.rsqrt(second - mean * mean + EPS_VAR)
    value = own[:1, :HALF] + own[:1, HALF:] + own[1:, :HALF]
    scaled = jnp.where(own[1:, HALF:] > 0.5, (value - mean) * scale, 0.0)
    reward_ref[...] = scaled[:, :slots]
    count_ref[...] = sum_of(slots + 2)[:, :1].astype(jnp.int32)


def fused(features, rewards, lengths, owners, norm_gain):
    row_count, width = features.shape[2:]
    games = lengths.shape[2]
    actors, groups = lax.axis_size("actors"), lax.axis_size("rep")
    slots = actors * CAP
    across = width // LANES
    last = CAP * across // PAIR
    order, place_of = places(actors, groups)
    vmem = pl.BlockSpec(memory_space=pltpu.VMEM)
    smem = pl.BlockSpec(memory_space=pltpu.SMEM)
    packed = pl.pallas_call(
        functools.partial(pack_kernel, place_of, groups),
        out_shape=jax.ShapeDtypeStruct((games * groups, last + 1, PAIR, LANES), jnp.bfloat16),
        in_specs=[smem, smem, smem, vmem, vmem, vmem],
        out_specs=vmem,
        scratch_shapes=[
            pltpu.VMEM(((across + 1) * row_count, LANES), jnp.float32),
            pltpu.VMEM((PAIR * games, LANES), jnp.float32),
            pltpu.SMEM((games,), jnp.int32),
            pltpu.SMEM((games,), jnp.int32),
        ],
        compiler_params=pltpu.CompilerParams(vmem_limit_bytes=VMEM_GRANT),
        name="pack",
    )(
        *(
            pltpu.with_memory_space_constraint(x, pltpu.HBM)
            for x in (
                lengths.reshape(1, games),
                owners.reshape(1, games),
                rewards.reshape(1, row_count),
                features.reshape(row_count, width),
                norm_gain.reshape(1, width),
                rewards.reshape(1, row_count),
            )
        )
    )
    landed = lax.all_to_all(
        packed, ("actors", "rep"), split_axis=0, concat_axis=0, tiled=True, axis_index_groups=[order]
    )
    rows, scaled, count = pl.pallas_call(
        functools.partial(unpack_kernel, place_of, groups, row_count * actors * groups),
        out_shape=(
            jax.ShapeDtypeStruct((slots, width), jnp.bfloat16),
            jax.ShapeDtypeStruct((1, slots), jnp.float32),
            jax.ShapeDtypeStruct((1, 1), jnp.int32),
        ),
        in_specs=[vmem],
        out_specs=(vmem, vmem, vmem),
        scratch_shapes=[
            pltpu.VMEM((slots * across, LANES), jnp.float32),
        ],
        compiler_params=pltpu.CompilerParams(vmem_limit_bytes=VMEM_GRANT),
        name="unpack",
    )(landed)
    return (rows.reshape(1, 1, -1, width), scaled.reshape(1, 1, -1), count.reshape(1))


def rms_scale(rows, norm_gain):
    widened = rows.astype(jnp.float32)
    square_mean = jnp.mean(widened * widened, axis=-1, keepdims=True)
    return (widened * lax.rsqrt(square_mean + EPS_NORM) * norm_gain).astype(jnp.bfloat16)


def plain(features, rewards, lengths, owners, norm_gain):
    rows_here = features[0, 0]
    reward_here = rewards[0, 0]
    game_len = lengths[0, 0]
    game_owner = owners[0, 0]
    games = game_len.shape[0]
    row_count = rows_here.shape[0]
    width = rows_here.shape[1]
    row_total = row_count * lax.axis_size("actors") * lax.axis_size("rep")
    starts = jnp.cumsum(game_len) - game_len
    trainer_ids = jnp.arange(games, dtype=jnp.int32)
    owns_game = (game_owner[None, :] == trainer_ids[:, None]).astype(jnp.int32)
    held_len = jnp.sum(owns_game * game_len[None, :], axis=1)
    held_start = jnp.sum(owns_game * starts[None, :], axis=1)
    slot_pos = jnp.arange(CAP, dtype=jnp.int32)
    usable = slot_pos[None, :] < held_len[:, None]
    row_index = jnp.minimum(held_start[:, None] + slot_pos[None, :], row_count - 1)
    outgoing = jnp.where(usable, jnp.take(reward_here, row_index, axis=0), jnp.zeros((), jnp.float32))
    outgoing = jnp.concatenate([outgoing, held_len.astype(jnp.float32)[:, None]], axis=1)
    arrived = lax.all_to_all(outgoing, "actors", split_axis=0, concat_axis=0, tiled=True)
    arrived, arrived_len = arrived[:, :CAP], arrived[:, CAP:]
    normed = rms_scale(rows_here, norm_gain)
    packed = jnp.where(usable[:, :, None], jnp.take(normed, row_index, axis=0), jnp.zeros((), jnp.bfloat16))
    landed = lax.all_to_all(packed, "actors", split_axis=0, concat_axis=0, tiled=True)
    first, second = lax.psum((jnp.sum(arrived), jnp.sum(arrived * arrived)), ("actors", "rep"))
    reward_mean = first / row_total
    inv_spread = lax.rsqrt(second / row_total - reward_mean * reward_mean + EPS_VAR)
    keep_slot = slot_pos[None, :].astype(jnp.float32) < arrived_len
    scaled = jnp.where(keep_slot, (arrived - reward_mean) * inv_spread, jnp.zeros((), jnp.float32))
    count_here = jnp.sum(arrived_len).astype(jnp.int32)
    counts = lax.psum(count_here, "rep")
    return (landed.reshape(1, 1, -1, width), scaled.reshape(1, 1, -1), counts.reshape(1))


def local(features, rewards, lengths, owners, norm_gain):
    actors, groups = lax.axis_size("actors"), lax.axis_size("rep")
    row_count, width = features.shape[2:]
    fits = (
        actors * CAP + 3 <= HALF
        and lengths.shape[2] == actors
        and actors % SUBLANES == 0
        and width % (SUBLANES * LANES) == 0
        and row_count % 16 == 0
        and row_count <= LANES
    )
    step = fused if fits else plain
    return step(features, rewards, lengths, owners, norm_gain)


def solution(mesh):
    return jax.shard_map(
        local,
        mesh=mesh,
        in_specs=(
            P("rep", "actors", None, None),
            P("rep", "actors", None),
            P("rep", "actors", None),
            P("rep", "actors", None),
            P(),
        ),
        out_specs=(P("rep", "actors", None, None), P("rep", "actors", None), P("actors")),
        check_vma=False,
    )
```

```python
import functools

import jax
import jax.numpy as jnp
from jax import lax
from jax.experimental import pallas as pl
from jax.experimental.pallas import tpu as pltpu
from jax.sharding import PartitionSpec as P

CAP = 3
EPS_NORM = 1e-06
EPS_VAR = 1e-05

LANES = 128
SUBLANES = 8
PAIR = 2
HALF = LANES // 2
VMEM_GRANT = 8 << 20
PARTS = 2
ORDERS = {(8, 4): [14, 0, 5, 3, 2, 11, 4, 1, 15, 9, 10, 6, 8, 13, 7, 12]}


def places(actors, groups):
    inner = groups // PARTS
    order = ORDERS.get((actors, groups)) or [a * inner + g for g in range(inner) for a in range(actors)]
    parts = [[d // inner * groups + d % inner * PARTS + part for d in order] for part in range(PARTS)]
    return parts, [order.index(device) for device in range(actors * inner)]


def of_group(choices, mine):
    chosen = jnp.int32(choices[0])
    for group in range(1, len(choices)):
        chosen = jnp.where(mine == group, choices[group], chosen)
    return chosen


def pack_kernel(
    place_of, groups, length_ref, owner_ref, reward_at, rows_ref, gain_ref, reward_ref,
    out_ref, normed_ref, scalar_ref, start_of, length_of,
):
    games = length_ref.shape[1]
    row_count, width = rows_ref.shape
    across = width // LANES
    stride = row_count
    last = out_ref.shape[1] - 1
    mine, actor = lax.axis_index("rep") // PARTS, lax.axis_index("actors")
    slots = lax.axis_size("actors") * CAP

    start = jnp.int32(0)
    for game in range(games):
        owner, size = owner_ref[0, game], length_ref[0, game]
        start_of[owner] = start
        length_of[owner] = size
        start = start + size

    wide = rows_ref[...].astype(jnp.float32)
    square_mean = jnp.sum(wide * wide, axis=1, keepdims=True) / width
    normed = wide * lax.rsqrt(square_mean + EPS_NORM) * gain_ref[...]
    for k in range(across):
        normed_ref[k * stride : k * stride + row_count] = normed[:, k * LANES : (k + 1) * LANES]

    lane = lax.broadcasted_iota(jnp.int32, (games, LANES), 1)
    place = lane % HALF
    trainer = lax.broadcasted_iota(jnp.int32, (games, LANES), 0)
    reward = reward_ref[...]
    first = jnp.sum(reward, axis=1, keepdims=True)
    second = jnp.sum(reward * reward, axis=1, keepdims=True)
    sizes = jnp.zeros((games, LANES), jnp.int32)
    held = [jnp.zeros((games, LANES), jnp.float32) for _ in range(CAP)]
    for t in range(games):
        begin, size = start_of[t], length_of[t]
        sizes = jnp.where(trainer == t, size, sizes)
        parts = []
        for j in range(CAP):
            part = normed_ref[pl.ds(begin + j, across, stride=stride), :]
            parts.append(jnp.where(j < size, part, 0.0))
            value = reward_at[0, jnp.minimum(begin + j, row_count - 1)]
            held[j] = jnp.where(trainer == t, value, held[j])
        block = jnp.concatenate(parts, axis=0).astype(jnp.bfloat16)
        target = of_group([place_of[t * groups + group] for group in range(groups)], mine)
        out_ref[target, :last] = block.reshape(last, PAIR, LANES)

    own = place - CAP * actor
    kept = (own >= 0) & (own < sizes)
    values = jnp.where(place == slots, first, jnp.where(place == slots + 1, second, 0.0))
    values = jnp.where(place == slots + 2, sizes.astype(jnp.float32), values)
    for j in range(CAP):
        values = jnp.where(kept & (own == j), held[j], values)
    high = values.astype(jnp.bfloat16).astype(jnp.float32)
    middle = (values - high).astype(jnp.bfloat16).astype(jnp.float32)
    low = values - high - middle
    scalar_ref[pl.ds(0, games, stride=PAIR), :] = jnp.where(lane < HALF, high, middle)
    scalar_ref[pl.ds(1, games, stride=PAIR), :] = jnp.where(lane < HALF, low, jnp.where(kept, 1.0, 0.0))
    tiles = scalar_ref[...].astype(jnp.bfloat16).reshape(games, PAIR, LANES)
    for t in range(games):
        for group in range(groups):
            out_ref[place_of[t * groups + group], last] = tiles[t]


def sum_kernel(place_of, groups, in_ref, every_ref, own_ref):
    actors = in_ref.shape[0] // groups
    last = in_ref.shape[1] - 1
    mine = lax.axis_index("rep") // PARTS

    def total(blocks):
        terms = [in_ref[block, last].astype(jnp.float32) for block in blocks]
        while len(terms) > 1:
            terms = [sum(terms[at : at + 2]) for at in range(0, len(terms), 2)]
        return terms[0]

    every_ref[...] = total(range(actors * groups))
    own_ref[...] = total([of_group(place_of[s * groups : (s + 1) * groups], mine) for s in range(actors)])


def rows_kernel(place_of, groups, in_ref, rows_ref, piece_ref):
    actors = in_ref.shape[0] // groups
    last = in_ref.shape[1] - 1
    slots, width = rows_ref.shape
    across = width // LANES
    mine = lax.axis_index("rep") // PARTS
    for s in range(actors):
        at = of_group(place_of[s * groups : (s + 1) * groups], mine)
        block = in_ref[at, :last].reshape(last * PAIR, LANES).astype(jnp.float32)
        piece_ref[s * last * PAIR : (s + 1) * last * PAIR] = block
    for k in range(across):
        lanes = piece_ref[pl.ds(k, slots, stride=across), :]
        rows_ref[:, k * LANES : (k + 1) * LANES] = lanes.astype(jnp.bfloat16)


def reward_kernel(rows_total, every_ref, other_ref, own_ref, reward_ref, count_ref):
    slots = reward_ref.shape[1]
    every, own = every_ref[...] + other_ref[...], own_ref[...]

    def sum_of(at):
        parts = (every[:1, at : at + 1], every[:1, HALF + at : HALF + at + 1], every[1:, at : at + 1])
        high, middle, low = (jnp.broadcast_to(part, (1, HALF)) for part in parts)
        return high + middle + low

    mean = sum_of(slots) / rows_total
    second = sum_of(slots + 1) / rows_total
    scale = lax.rsqrt(second - mean * mean + EPS_VAR)
    value = own[:1, :HALF] + own[:1, HALF:] + own[1:, :HALF]
    scaled = jnp.where(own[1:, HALF:] > 0.5, (value - mean) * scale, 0.0)
    reward_ref[...] = scaled[:, :slots]
    count_ref[...] = sum_of(slots + 2)[:, :1].astype(jnp.int32)


def fused(features, rewards, lengths, owners, norm_gain):
    row_count, width = features.shape[2:]
    games = lengths.shape[2]
    actors, groups = lax.axis_size("actors"), lax.axis_size("rep")
    slots = actors * CAP
    across = width // LANES
    last = CAP * across // PAIR
    parts, place_of = places(actors, groups)
    inner = groups // PARTS
    tile = jax.ShapeDtypeStruct((PAIR, LANES), jnp.float32)
    params = pltpu.CompilerParams(vmem_limit_bytes=VMEM_GRANT)
    vmem = pl.BlockSpec(memory_space=pltpu.VMEM)
    smem = pl.BlockSpec(memory_space=pltpu.SMEM)
    packed = pl.pallas_call(
        functools.partial(pack_kernel, place_of, inner),
        out_shape=jax.ShapeDtypeStruct((games * inner, last + 1, PAIR, LANES), jnp.bfloat16),
        in_specs=[smem, smem, smem, vmem, vmem, vmem],
        out_specs=vmem,
        scratch_shapes=[
            pltpu.VMEM(((across + 1) * row_count, LANES), jnp.float32),
            pltpu.VMEM((PAIR * games, LANES), jnp.float32),
            pltpu.SMEM((games,), jnp.int32),
            pltpu.SMEM((games,), jnp.int32),
        ],
        compiler_params=params,
        name="pack",
    )(
        *(
            pltpu.with_memory_space_constraint(x, pltpu.HBM)
            for x in (
                lengths.reshape(1, games),
                owners.reshape(1, games),
                rewards.reshape(1, row_count),
                features.reshape(row_count, width),
                norm_gain.reshape(1, width),
                rewards.reshape(1, row_count),
            )
        )
    )
    landed = lax.all_to_all(
        packed, ("actors", "rep"), split_axis=0, concat_axis=0, tiled=True, axis_index_groups=parts
    )
    every, own = pl.pallas_call(
        functools.partial(sum_kernel, place_of, inner),
        out_shape=(tile, tile),
        in_specs=[vmem],
        out_specs=(vmem, vmem),
        compiler_params=params,
        name="sums",
    )(landed)
    others = [(group, group // PARTS * PARTS + (group + 1) % PARTS) for group in range(groups)]
    other = lax.ppermute(every, "rep", others)
    rows = pl.pallas_call(
        functools.partial(rows_kernel, place_of, inner),
        out_shape=jax.ShapeDtypeStruct((slots, width), jnp.bfloat16),
        in_specs=[vmem],
        out_specs=vmem,
        scratch_shapes=[pltpu.VMEM((slots * across, LANES), jnp.float32)],
        compiler_params=params,
        name="rows",
    )(landed)
    scaled, count = pl.pallas_call(
        functools.partial(reward_kernel, row_count * actors * groups),
        out_shape=(jax.ShapeDtypeStruct((1, slots), jnp.float32), jax.ShapeDtypeStruct((1, 1), jnp.int32)),
        in_specs=[vmem, vmem, vmem],
        out_specs=(vmem, vmem),
        compiler_params=params,
        name="rewards",
    )(every, other, own)
    return (rows.reshape(1, 1, -1, width), scaled.reshape(1, 1, -1), count.reshape(1))


def rms_scale(rows, norm_gain):
    widened = rows.astype(jnp.float32)
    square_mean = jnp.mean(widened * widened, axis=-1, keepdims=True)
    return (widened * lax.rsqrt(square_mean + EPS_NORM) * norm_gain).astype(jnp.bfloat16)


def plain(features, rewards, lengths, owners, norm_gain):
    rows_here = features[0, 0]
    reward_here = rewards[0, 0]
    game_len = lengths[0, 0]
    game_owner = owners[0, 0]
    games = game_len.shape[0]
    row_count = rows_here.shape[0]
    width = rows_here.shape[1]
    row_total = row_count * lax.axis_size("actors") * lax.axis_size("rep")
    starts = jnp.cumsum(game_len) - game_len
    trainer_ids = jnp.arange(games, dtype=jnp.int32)
    owns_game = (game_owner[None, :] == trainer_ids[:, None]).astype(jnp.int32)
    held_len = jnp.sum(owns_game * game_len[None, :], axis=1)
    held_start = jnp.sum(owns_game * starts[None, :], axis=1)
    slot_pos = jnp.arange(CAP, dtype=jnp.int32)
    usable = slot_pos[None, :] < held_len[:, None]
    row_index = jnp.minimum(held_start[:, None] + slot_pos[None, :], row_count - 1)
    outgoing = jnp.where(usable, jnp.take(reward_here, row_index, axis=0), jnp.zeros((), jnp.float32))
    outgoing = jnp.concatenate([outgoing, held_len.astype(jnp.float32)[:, None]], axis=1)
    arrived = lax.all_to_all(outgoing, "actors", split_axis=0, concat_axis=0, tiled=True)
    arrived, arrived_len = arrived[:, :CAP], arrived[:, CAP:]
    normed = rms_scale(rows_here, norm_gain)
    packed = jnp.where(usable[:, :, None], jnp.take(normed, row_index, axis=0), jnp.zeros((), jnp.bfloat16))
    landed = lax.all_to_all(packed, "actors", split_axis=0, concat_axis=0, tiled=True)
    first, second = lax.psum((jnp.sum(arrived), jnp.sum(arrived * arrived)), ("actors", "rep"))
    reward_mean = first / row_total
    inv_spread = lax.rsqrt(second / row_total - reward_mean * reward_mean + EPS_VAR)
    keep_slot = slot_pos[None, :].astype(jnp.float32) < arrived_len
    scaled = jnp.where(keep_slot, (arrived - reward_mean) * inv_spread, jnp.zeros((), jnp.float32))
    count_here = jnp.sum(arrived_len).astype(jnp.int32)
    counts = lax.psum(count_here, "rep")
    return (landed.reshape(1, 1, -1, width), scaled.reshape(1, 1, -1), counts.reshape(1))


def local(features, rewards, lengths, owners, norm_gain):
    actors, groups = lax.axis_size("actors"), lax.axis_size("rep")
    row_count, width = features.shape[2:]
    fits = (
        actors * CAP + 3 <= HALF
        and lengths.shape[2] == actors
        and groups % PARTS == 0
        and actors % SUBLANES == 0
        and width % (SUBLANES * LANES) == 0
        and row_count % 16 == 0
        and row_count <= LANES
    )
    step = fused if fits else plain
    return step(features, rewards, lengths, owners, norm_gain)


def solution(mesh):
    return jax.shard_map(
        local,
        mesh=mesh,
        in_specs=(
            P("rep", "actors", None, None),
            P("rep", "actors", None),
            P("rep", "actors", None),
            P("rep", "actors", None),
            P(),
        ),
        out_specs=(P("rep", "actors", None, None), P("rep", "actors", None), P("actors")),
        check_vma=False,
    )
```

```python
import functools

import jax
import jax.numpy as jnp
from jax import lax
from jax.experimental import pallas as pl
from jax.experimental.pallas import tpu as pltpu
from jax.sharding import PartitionSpec as P

CAP = 3
EPS_NORM = 1e-06
EPS_VAR = 1e-05

LANES = 128
SUBLANES = 8
PAIR = 2
HALF = LANES // 2
VMEM_GRANT = 8 << 20
PARTS = 2
ORDERS = {(8, 4): [14, 0, 5, 3, 2, 11, 4, 1, 15, 9, 10, 6, 8, 13, 7, 12]}


def places(actors, groups):
    inner = groups // PARTS
    order = ORDERS.get((actors, groups)) or [a * inner + g for g in range(inner) for a in range(actors)]
    parts = [[d // inner * groups + d % inner * PARTS + part for d in order] for part in range(PARTS)]
    return parts, [order.index(device) for device in range(actors * inner)]


def of_group(choices, mine):
    chosen = jnp.int32(choices[0])
    for group in range(1, len(choices)):
        chosen = jnp.where(mine == group, choices[group], chosen)
    return chosen


def pack_kernel(
    place_of, groups, length_ref, owner_ref, reward_at, rows_ref, gain_ref, reward_ref,
    out_ref, normed_ref, scalar_ref, start_of, length_of,
):
    games = length_ref.shape[1]
    row_count, width = rows_ref.shape
    across = width // LANES
    stride = row_count
    last = out_ref.shape[1] - 1
    mine, actor = lax.axis_index("rep") // PARTS, lax.axis_index("actors")
    slots = lax.axis_size("actors") * CAP

    start = jnp.int32(0)
    for game in range(games):
        owner, size = owner_ref[0, game], length_ref[0, game]
        start_of[owner] = start
        length_of[owner] = size
        start = start + size

    wide = rows_ref[...].astype(jnp.float32)
    square_mean = jnp.sum(wide * wide, axis=1, keepdims=True) / width
    normed = wide * lax.rsqrt(square_mean + EPS_NORM) * gain_ref[...]
    for k in range(across):
        normed_ref[k * stride : k * stride + row_count] = normed[:, k * LANES : (k + 1) * LANES]

    lane = lax.broadcasted_iota(jnp.int32, (games, LANES), 1)
    place = lane % HALF
    trainer = lax.broadcasted_iota(jnp.int32, (games, LANES), 0)
    reward = reward_ref[...]
    first = jnp.sum(reward, axis=1, keepdims=True)
    second = jnp.sum(reward * reward, axis=1, keepdims=True)
    sizes = jnp.zeros((games, LANES), jnp.int32)
    held = [jnp.zeros((games, LANES), jnp.float32) for _ in range(CAP)]
    for t in range(games):
        begin, size = start_of[t], length_of[t]
        sizes = jnp.where(trainer == t, size, sizes)
        parts = []
        for j in range(CAP):
            part = normed_ref[pl.ds(begin + j, across, stride=stride), :]
            parts.append(jnp.where(j < size, part, 0.0))
            value = reward_at[0, jnp.minimum(begin + j, row_count - 1)]
            held[j] = jnp.where(trainer == t, value, held[j])
        block = jnp.concatenate(parts, axis=0).astype(jnp.bfloat16)
        target = of_group([place_of[t * groups + group] for group in range(groups)], mine)
        out_ref[target, :last] = block.reshape(last, PAIR, LANES)

    own = place - CAP * actor
    kept = (own >= 0) & (own < sizes)
    values = jnp.where(place == slots, first, jnp.where(place == slots + 1, second, 0.0))
    values = jnp.where(place == slots + 2, sizes.astype(jnp.float32), values)
    for j in range(CAP):
        values = jnp.where(kept & (own == j), held[j], values)
    high = values.astype(jnp.bfloat16).astype(jnp.float32)
    middle = (values - high).astype(jnp.bfloat16).astype(jnp.float32)
    low = values - high - middle
    scalar_ref[pl.ds(0, games, stride=PAIR), :] = jnp.where(lane < HALF, high, middle)
    scalar_ref[pl.ds(1, games, stride=PAIR), :] = jnp.where(lane < HALF, low, jnp.where(kept, 1.0, 0.0))
    tiles = scalar_ref[...].astype(jnp.bfloat16).reshape(games, PAIR, LANES)
    for t in range(games):
        for group in range(groups):
            out_ref[place_of[t * groups + group], last] = tiles[t]


def sum_kernel(place_of, groups, in_ref, every_ref, own_ref):
    actors = in_ref.shape[0] // groups
    last = in_ref.shape[1] - 1
    mine = lax.axis_index("rep") // PARTS

    def total(blocks):
        terms = [in_ref[block, last].astype(jnp.float32) for block in blocks]
        while len(terms) > 1:
            terms = [sum(terms[at : at + 2]) for at in range(0, len(terms), 2)]
        return terms[0]

    every = total(range(actors * groups))
    slots = actors * CAP
    every_ref[...] = jnp.zeros_like(every_ref)
    own_ref[...] = jnp.zeros_like(own_ref)
    for n in range(3):
        at = slots + n
        parts = (every[:1, at : at + 1], every[:1, HALF + at : HALF + at + 1], every[1:, at : at + 1])
        high, middle, low = (jnp.broadcast_to(part, (1, LANES)) for part in parts)
        every_ref[n : n + 1] = high + middle + low
    own = total([of_group(place_of[s * groups : (s + 1) * groups], mine) for s in range(actors)])
    own_ref[:1, :HALF] = own[:1, :HALF] + own[:1, HALF:] + own[1:, :HALF]
    own_ref[1:2, :HALF] = own[1:, HALF:]


def rows_kernel(place_of, groups, in_ref, rows_ref, piece_ref):
    actors = in_ref.shape[0] // groups
    last = in_ref.shape[1] - 1
    slots, width = rows_ref.shape
    across = width // LANES
    mine = lax.axis_index("rep") // PARTS
    for s in range(actors):
        at = of_group(place_of[s * groups : (s + 1) * groups], mine)
        block = in_ref[at, :last].reshape(last * PAIR, LANES).astype(jnp.float32)
        piece_ref[s * last * PAIR : (s + 1) * last * PAIR] = block
    for k in range(across):
        lanes = piece_ref[pl.ds(k, slots, stride=across), :]
        rows_ref[:, k * LANES : (k + 1) * LANES] = lanes.astype(jnp.bfloat16)


def reward_kernel(rows_total, every_ref, other_ref, own_ref, reward_ref, count_ref):
    slots = reward_ref.shape[1]
    every = every_ref[...] + other_ref[...]
    mean, second = every[:1] / rows_total, every[1:2] / rows_total
    scale = lax.rsqrt(second - mean * mean + EPS_VAR)
    scaled = jnp.where(own_ref[1:2] > 0.5, (own_ref[:1] - mean) * scale, 0.0)
    reward_ref[...] = scaled[:, :slots]
    count_ref[...] = every[2:3, :1].astype(jnp.int32)


def fused(features, rewards, lengths, owners, norm_gain):
    row_count, width = features.shape[2:]
    games = lengths.shape[2]
    actors, groups = lax.axis_size("actors"), lax.axis_size("rep")
    slots = actors * CAP
    across = width // LANES
    last = CAP * across // PAIR
    parts, place_of = places(actors, groups)
    inner = groups // PARTS
    tile = jax.ShapeDtypeStruct((SUBLANES, LANES), jnp.float32)
    params = pltpu.CompilerParams(vmem_limit_bytes=VMEM_GRANT)
    vmem = pl.BlockSpec(memory_space=pltpu.VMEM)
    smem = pl.BlockSpec(memory_space=pltpu.SMEM)
    packed = pl.pallas_call(
        functools.partial(pack_kernel, place_of, inner),
        out_shape=jax.ShapeDtypeStruct((games * inner, last + 1, PAIR, LANES), jnp.bfloat16),
        in_specs=[smem, smem, smem, vmem, vmem, vmem],
        out_specs=vmem,
        scratch_shapes=[
            pltpu.VMEM(((across + 1) * row_count, LANES), jnp.float32),
            pltpu.VMEM((PAIR * games, LANES), jnp.float32),
            pltpu.SMEM((games,), jnp.int32),
            pltpu.SMEM((games,), jnp.int32),
        ],
        compiler_params=params,
        name="pack",
    )(
        *(
            pltpu.with_memory_space_constraint(x, pltpu.HBM)
            for x in (
                lengths.reshape(1, games),
                owners.reshape(1, games),
                rewards.reshape(1, row_count),
                features.reshape(row_count, width),
                norm_gain.reshape(1, width),
                rewards.reshape(1, row_count),
            )
        )
    )
    landed = lax.all_to_all(
        packed, ("actors", "rep"), split_axis=0, concat_axis=0, tiled=True, axis_index_groups=parts
    )
    every, own = pl.pallas_call(
        functools.partial(sum_kernel, place_of, inner),
        out_shape=(tile, tile),
        in_specs=[vmem],
        out_specs=(vmem, vmem),
        compiler_params=params,
        name="sums",
    )(landed)
    others = [(group, group // PARTS * PARTS + (group + 1) % PARTS) for group in range(groups)]
    other = lax.ppermute(every, "rep", others)
    rows = pl.pallas_call(
        functools.partial(rows_kernel, place_of, inner),
        out_shape=jax.ShapeDtypeStruct((slots, width), jnp.bfloat16),
        in_specs=[vmem],
        out_specs=vmem,
        scratch_shapes=[pltpu.VMEM((slots * across, LANES), jnp.float32)],
        compiler_params=params,
        name="rows",
    )(landed)
    scaled, count = pl.pallas_call(
        functools.partial(reward_kernel, row_count * actors * groups),
        out_shape=(jax.ShapeDtypeStruct((1, slots), jnp.float32), jax.ShapeDtypeStruct((1, 1), jnp.int32)),
        in_specs=[vmem, vmem, vmem],
        out_specs=(vmem, vmem),
        compiler_params=params,
        name="rewards",
    )(every, other, own)
    return (rows.reshape(1, 1, -1, width), scaled.reshape(1, 1, -1), count.reshape(1))


def rms_scale(rows, norm_gain):
    widened = rows.astype(jnp.float32)
    square_mean = jnp.mean(widened * widened, axis=-1, keepdims=True)
    return (widened * lax.rsqrt(square_mean + EPS_NORM) * norm_gain).astype(jnp.bfloat16)


def plain(features, rewards, lengths, owners, norm_gain):
    rows_here = features[0, 0]
    reward_here = rewards[0, 0]
    game_len = lengths[0, 0]
    game_owner = owners[0, 0]
    games = game_len.shape[0]
    row_count = rows_here.shape[0]
    width = rows_here.shape[1]
    row_total = row_count * lax.axis_size("actors") * lax.axis_size("rep")
    starts = jnp.cumsum(game_len) - game_len
    trainer_ids = jnp.arange(games, dtype=jnp.int32)
    owns_game = (game_owner[None, :] == trainer_ids[:, None]).astype(jnp.int32)
    held_len = jnp.sum(owns_game * game_len[None, :], axis=1)
    held_start = jnp.sum(owns_game * starts[None, :], axis=1)
    slot_pos = jnp.arange(CAP, dtype=jnp.int32)
    usable = slot_pos[None, :] < held_len[:, None]
    row_index = jnp.minimum(held_start[:, None] + slot_pos[None, :], row_count - 1)
    outgoing = jnp.where(usable, jnp.take(reward_here, row_index, axis=0), jnp.zeros((), jnp.float32))
    outgoing = jnp.concatenate([outgoing, held_len.astype(jnp.float32)[:, None]], axis=1)
    arrived = lax.all_to_all(outgoing, "actors", split_axis=0, concat_axis=0, tiled=True)
    arrived, arrived_len = arrived[:, :CAP], arrived[:, CAP:]
    normed = rms_scale(rows_here, norm_gain)
    packed = jnp.where(usable[:, :, None], jnp.take(normed, row_index, axis=0), jnp.zeros((), jnp.bfloat16))
    landed = lax.all_to_all(packed, "actors", split_axis=0, concat_axis=0, tiled=True)
    first, second = lax.psum((jnp.sum(arrived), jnp.sum(arrived * arrived)), ("actors", "rep"))
    reward_mean = first / row_total
    inv_spread = lax.rsqrt(second / row_total - reward_mean * reward_mean + EPS_VAR)
    keep_slot = slot_pos[None, :].astype(jnp.float32) < arrived_len
    scaled = jnp.where(keep_slot, (arrived - reward_mean) * inv_spread, jnp.zeros((), jnp.float32))
    count_here = jnp.sum(arrived_len).astype(jnp.int32)
    counts = lax.psum(count_here, "rep")
    return (landed.reshape(1, 1, -1, width), scaled.reshape(1, 1, -1), counts.reshape(1))


def local(features, rewards, lengths, owners, norm_gain):
    actors, groups = lax.axis_size("actors"), lax.axis_size("rep")
    row_count, width = features.shape[2:]
    fits = (
        actors * CAP + 3 <= HALF
        and lengths.shape[2] == actors
        and groups % PARTS == 0
        and actors % SUBLANES == 0
        and width % (SUBLANES * LANES) == 0
        and row_count % 16 == 0
        and row_count <= LANES
    )
    step = fused if fits else plain
    return step(features, rewards, lengths, owners, norm_gain)


def solution(mesh):
    return jax.shard_map(
        local,
        mesh=mesh,
        in_specs=(
            P("rep", "actors", None, None),
            P("rep", "actors", None),
            P("rep", "actors", None),
            P("rep", "actors", None),
            P(),
        ),
        out_specs=(P("rep", "actors", None, None), P("rep", "actors", None), P("actors")),
        check_vma=False,
    )
```

```python
import functools

import jax
import jax.numpy as jnp
from jax import lax
from jax.experimental import pallas as pl
from jax.experimental.pallas import tpu as pltpu
from jax.sharding import PartitionSpec as P

CAP = 3
EPS_NORM = 1e-06
EPS_VAR = 1e-05

LANES = 128
SUBLANES = 8
PAIR = 2
HALF = LANES // 2
VMEM_GRANT = 8 << 20
PARTS = 2
ORDERS = {(8, 4): [11, 7, 6, 3, 8, 4, 15, 14, 12, 10, 2, 0, 1, 5, 9, 13]}


def places(actors, groups):
    inner = groups // PARTS
    order = ORDERS.get((actors, groups)) or [a * inner + g for g in range(inner) for a in range(actors)]
    parts = [[d // inner * groups + d % inner * PARTS + part for d in order] for part in range(PARTS)]
    return parts, [order.index(device) for device in range(actors * inner)]


def of_group(choices, mine):
    chosen = jnp.int32(choices[0])
    for group in range(1, len(choices)):
        chosen = jnp.where(mine == group, choices[group], chosen)
    return chosen


def pack_kernel(
    place_of, groups, length_ref, owner_ref, reward_at, rows_ref, gain_ref, reward_ref,
    out_ref, normed_ref, scalar_ref, start_of, length_of,
):
    games = length_ref.shape[1]
    row_count, width = rows_ref.shape
    across = width // LANES
    stride = row_count
    last = out_ref.shape[1] - 1
    mine, actor = lax.axis_index("rep") // PARTS, lax.axis_index("actors")
    slots = lax.axis_size("actors") * CAP

    start = jnp.int32(0)
    for game in range(games):
        owner, size = owner_ref[0, game], length_ref[0, game]
        start_of[owner] = start
        length_of[owner] = size
        start = start + size

    wide = rows_ref[...].astype(jnp.float32)
    square_mean = jnp.sum(wide * wide, axis=1, keepdims=True) / width
    normed = wide * lax.rsqrt(square_mean + EPS_NORM) * gain_ref[...]
    for k in range(across):
        normed_ref[k * stride : k * stride + row_count] = normed[:, k * LANES : (k + 1) * LANES]

    lane = lax.broadcasted_iota(jnp.int32, (games, LANES), 1)
    place = lane % HALF
    trainer = lax.broadcasted_iota(jnp.int32, (games, LANES), 0)
    reward = reward_ref[...]
    first = jnp.sum(reward, axis=1, keepdims=True)
    second = jnp.sum(reward * reward, axis=1, keepdims=True)
    sizes = jnp.zeros((games, LANES), jnp.int32)
    held = [jnp.zeros((games, LANES), jnp.float32) for _ in range(CAP)]
    for t in range(games):
        begin, size = start_of[t], length_of[t]
        sizes = jnp.where(trainer == t, size, sizes)
        parts = []
        for j in range(CAP):
            part = normed_ref[pl.ds(begin + j, across, stride=stride), :]
            parts.append(jnp.where(j < size, part, 0.0))
            value = reward_at[0, jnp.minimum(begin + j, row_count - 1)]
            held[j] = jnp.where(trainer == t, value, held[j])
        block = jnp.concatenate(parts, axis=0).astype(jnp.bfloat16)
        target = of_group([place_of[t * groups + group] for group in range(groups)], mine)
        out_ref[target, :last] = block.reshape(last, PAIR, LANES)

    own = place - CAP * actor
    kept = (own >= 0) & (own < sizes)
    values = jnp.where(place == slots, first, jnp.where(place == slots + 1, second, 0.0))
    values = jnp.where(place == slots + 2, sizes.astype(jnp.float32), values)
    for j in range(CAP):
        values = jnp.where(kept & (own == j), held[j], values)
    high = values.astype(jnp.bfloat16).astype(jnp.float32)
    middle = (values - high).astype(jnp.bfloat16).astype(jnp.float32)
    low = values - high - middle
    scalar_ref[pl.ds(0, games, stride=PAIR), :] = jnp.where(lane < HALF, high, middle)
    scalar_ref[pl.ds(1, games, stride=PAIR), :] = jnp.where(lane < HALF, low, jnp.where(kept, 1.0, 0.0))
    tiles = scalar_ref[...].astype(jnp.bfloat16).reshape(games, PAIR, LANES)
    for t in range(games):
        for group in range(groups):
            out_ref[place_of[t * groups + group], last] = tiles[t]


def total(in_ref, blocks):
    terms = [in_ref[block, in_ref.shape[1] - 1].astype(jnp.float32) for block in blocks]
    while len(terms) > 1:
        terms = [sum(terms[at : at + 2]) for at in range(0, len(terms), 2)]
    return terms[0]


def sum_kernel(slots, in_ref, every_ref):
    every = total(in_ref, range(in_ref.shape[0]))
    every_ref[...] = jnp.zeros_like(every_ref)
    for n in range(3):
        at = slots + n
        parts = (every[:1, at : at + 1], every[:1, HALF + at : HALF + at + 1], every[1:, at : at + 1])
        high, middle, low = (jnp.broadcast_to(part, (1, LANES)) for part in parts)
        every_ref[n : n + 1] = high + middle + low


def rows_kernel(place_of, groups, in_ref, rows_ref, own_ref, piece_ref):
    actors = in_ref.shape[0] // groups
    last = in_ref.shape[1] - 1
    slots, width = rows_ref.shape
    across = width // LANES
    mine = lax.axis_index("rep") // PARTS
    own_places = [of_group(place_of[s * groups : (s + 1) * groups], mine) for s in range(actors)]
    for s, at in enumerate(own_places):
        block = in_ref[at, :last].reshape(last * PAIR, LANES).astype(jnp.float32)
        piece_ref[s * last * PAIR : (s + 1) * last * PAIR] = block
    for k in range(across):
        lanes = piece_ref[pl.ds(k, slots, stride=across), :]
        rows_ref[:, k * LANES : (k + 1) * LANES] = lanes.astype(jnp.bfloat16)
    own = total(in_ref, own_places)
    own_ref[...] = jnp.zeros_like(own_ref)
    own_ref[:1, :HALF] = own[:1, :HALF] + own[:1, HALF:] + own[1:, :HALF]
    own_ref[1:2, :HALF] = own[1:, HALF:]


def reward_kernel(rows_total, every_ref, other_ref, own_ref, reward_ref, count_ref):
    slots = reward_ref.shape[1]
    every = every_ref[...] + other_ref[...]
    mean, second = every[:1] / rows_total, every[1:2] / rows_total
    scale = lax.rsqrt(second - mean * mean + EPS_VAR)
    scaled = jnp.where(own_ref[1:2] > 0.5, (own_ref[:1] - mean) * scale, 0.0)
    reward_ref[...] = scaled[:, :slots]
    count_ref[...] = every[2:3, :1].astype(jnp.int32)


def fused(features, rewards, lengths, owners, norm_gain):
    row_count, width = features.shape[2:]
    games = lengths.shape[2]
    actors, groups = lax.axis_size("actors"), lax.axis_size("rep")
    slots = actors * CAP
    across = width // LANES
    last = CAP * across // PAIR
    parts, place_of = places(actors, groups)
    inner = groups // PARTS
    tile = jax.ShapeDtypeStruct((SUBLANES, LANES), jnp.float32)
    params = pltpu.CompilerParams(vmem_limit_bytes=VMEM_GRANT)
    vmem = pl.BlockSpec(memory_space=pltpu.VMEM)
    smem = pl.BlockSpec(memory_space=pltpu.SMEM)
    packed = pl.pallas_call(
        functools.partial(pack_kernel, place_of, inner),
        out_shape=jax.ShapeDtypeStruct((games * inner, last + 1, PAIR, LANES), jnp.bfloat16),
        in_specs=[smem, smem, smem, vmem, vmem, vmem],
        out_specs=vmem,
        scratch_shapes=[
            pltpu.VMEM(((across + 1) * row_count, LANES), jnp.float32),
            pltpu.VMEM((PAIR * games, LANES), jnp.float32),
            pltpu.SMEM((games,), jnp.int32),
            pltpu.SMEM((games,), jnp.int32),
        ],
        compiler_params=params,
        name="pack",
    )(
        *(
            pltpu.with_memory_space_constraint(x, pltpu.HBM)
            for x in (
                lengths.reshape(1, games),
                owners.reshape(1, games),
                rewards.reshape(1, row_count),
                features.reshape(row_count, width),
                norm_gain.reshape(1, width),
                rewards.reshape(1, row_count),
            )
        )
    )
    landed = lax.all_to_all(
        packed, ("actors", "rep"), split_axis=0, concat_axis=0, tiled=True, axis_index_groups=parts
    )
    every = pl.pallas_call(
        functools.partial(sum_kernel, slots),
        out_shape=tile,
        in_specs=[vmem],
        out_specs=vmem,
        compiler_params=params,
        name="sums",
    )(landed)
    others = [(group, group // PARTS * PARTS + (group + 1) % PARTS) for group in range(groups)]
    other = lax.ppermute(every, "rep", others)
    rows, own = pl.pallas_call(
        functools.partial(rows_kernel, place_of, inner),
        out_shape=(jax.ShapeDtypeStruct((slots, width), jnp.bfloat16), tile),
        in_specs=[vmem],
        out_specs=(vmem, vmem),
        scratch_shapes=[pltpu.VMEM((slots * across, LANES), jnp.float32)],
        compiler_params=params,
        name="rows",
    )(landed)
    scaled, count = pl.pallas_call(
        functools.partial(reward_kernel, row_count * actors * groups),
        out_shape=(jax.ShapeDtypeStruct((1, slots), jnp.float32), jax.ShapeDtypeStruct((1, 1), jnp.int32)),
        in_specs=[vmem, vmem, vmem],
        out_specs=(vmem, vmem),
        compiler_params=params,
        name="rewards",
    )(every, other, own)
    return (rows.reshape(1, 1, -1, width), scaled.reshape(1, 1, -1), count.reshape(1))


def rms_scale(rows, norm_gain):
    widened = rows.astype(jnp.float32)
    square_mean = jnp.mean(widened * widened, axis=-1, keepdims=True)
    return (widened * lax.rsqrt(square_mean + EPS_NORM) * norm_gain).astype(jnp.bfloat16)


def plain(features, rewards, lengths, owners, norm_gain):
    rows_here = features[0, 0]
    reward_here = rewards[0, 0]
    game_len = lengths[0, 0]
    game_owner = owners[0, 0]
    games = game_len.shape[0]
    row_count = rows_here.shape[0]
    width = rows_here.shape[1]
    row_total = row_count * lax.axis_size("actors") * lax.axis_size("rep")
    starts = jnp.cumsum(game_len) - game_len
    trainer_ids = jnp.arange(games, dtype=jnp.int32)
    owns_game = (game_owner[None, :] == trainer_ids[:, None]).astype(jnp.int32)
    held_len = jnp.sum(owns_game * game_len[None, :], axis=1)
    held_start = jnp.sum(owns_game * starts[None, :], axis=1)
    slot_pos = jnp.arange(CAP, dtype=jnp.int32)
    usable = slot_pos[None, :] < held_len[:, None]
    row_index = jnp.minimum(held_start[:, None] + slot_pos[None, :], row_count - 1)
    outgoing = jnp.where(usable, jnp.take(reward_here, row_index, axis=0), jnp.zeros((), jnp.float32))
    outgoing = jnp.concatenate([outgoing, held_len.astype(jnp.float32)[:, None]], axis=1)
    arrived = lax.all_to_all(outgoing, "actors", split_axis=0, concat_axis=0, tiled=True)
    arrived, arrived_len = arrived[:, :CAP], arrived[:, CAP:]
    normed = rms_scale(rows_here, norm_gain)
    packed = jnp.where(usable[:, :, None], jnp.take(normed, row_index, axis=0), jnp.zeros((), jnp.bfloat16))
    landed = lax.all_to_all(packed, "actors", split_axis=0, concat_axis=0, tiled=True)
    first, second = lax.psum((jnp.sum(arrived), jnp.sum(arrived * arrived)), ("actors", "rep"))
    reward_mean = first / row_total
    inv_spread = lax.rsqrt(second / row_total - reward_mean * reward_mean + EPS_VAR)
    keep_slot = slot_pos[None, :].astype(jnp.float32) < arrived_len
    scaled = jnp.where(keep_slot, (arrived - reward_mean) * inv_spread, jnp.zeros((), jnp.float32))
    count_here = jnp.sum(arrived_len).astype(jnp.int32)
    counts = lax.psum(count_here, "rep")
    return (landed.reshape(1, 1, -1, width), scaled.reshape(1, 1, -1), counts.reshape(1))


def local(features, rewards, lengths, owners, norm_gain):
    actors, groups = lax.axis_size("actors"), lax.axis_size("rep")
    row_count, width = features.shape[2:]
    fits = (
        actors * CAP + 3 <= HALF
        and lengths.shape[2] == actors
        and groups % PARTS == 0
        and actors % SUBLANES == 0
        and width % (SUBLANES * LANES) == 0
        and row_count % 16 == 0
        and row_count <= LANES
    )
    step = fused if fits else plain
    return step(features, rewards, lengths, owners, norm_gain)


def solution(mesh):
    return jax.shard_map(
        local,
        mesh=mesh,
        in_specs=(
            P("rep", "actors", None, None),
            P("rep", "actors", None),
            P("rep", "actors", None),
            P("rep", "actors", None),
            P(),
        ),
        out_specs=(P("rep", "actors", None, None), P("rep", "actors", None), P("actors")),
        check_vma=False,
    )
```

```python
import functools

import jax
import jax.numpy as jnp
from jax import lax
from jax.experimental import pallas as pl
from jax.experimental.pallas import tpu as pltpu
from jax.sharding import PartitionSpec as P

CAP = 3
EPS_NORM = 1e-06
EPS_VAR = 1e-05

LANES = 128
SUBLANES = 8
PAIR = 2
HALF = LANES // 2
VMEM_GRANT = 8 << 20
PARTS = 2
ORDERS = {(8, 4): [11, 7, 6, 3, 8, 4, 15, 14, 12, 10, 2, 0, 1, 5, 9, 13]}


def places(actors, groups):
    inner = groups // PARTS
    order = ORDERS.get((actors, groups)) or [a * inner + g for g in range(inner) for a in range(actors)]
    parts = [[d // inner * groups + d % inner * PARTS + part for d in order] for part in range(PARTS)]
    return parts, [order.index(device) for device in range(actors * inner)]


def of_group(choices, mine):
    chosen = jnp.int32(choices[0])
    for group in range(1, len(choices)):
        chosen = jnp.where(mine == group, choices[group], chosen)
    return chosen


def pack_kernel(
    place_of, groups, length_ref, owner_ref, reward_at, rows_ref, gain_ref, reward_ref,
    out_ref, wide_ref, scale_ref, scalar_ref, start_of, length_of,
):
    games = length_ref.shape[1]
    row_count, width = rows_ref.shape
    across = width // LANES
    stride = row_count
    last = out_ref.shape[1] - 1
    mine, actor = lax.axis_index("rep") // PARTS, lax.axis_index("actors")
    slots = lax.axis_size("actors") * CAP

    start = jnp.int32(0)
    for game in range(games):
        owner, size = owner_ref[0, game], length_ref[0, game]
        start_of[owner] = start
        length_of[owner] = size
        start = start + size

    wide = rows_ref[...].astype(jnp.float32)
    for k in range(across):
        wide_ref[k * stride : k * stride + row_count] = wide[:, k * LANES : (k + 1) * LANES]
    square_mean = jnp.sum(wide * wide, axis=1, keepdims=True) / width
    scale_ref[:row_count] = jnp.broadcast_to(lax.rsqrt(square_mean + EPS_NORM), (row_count, LANES))
    gain = gain_ref[...]

    lane = lax.broadcasted_iota(jnp.int32, (games, LANES), 1)
    place = lane % HALF
    trainer = lax.broadcasted_iota(jnp.int32, (games, LANES), 0)
    reward = reward_ref[...]
    first = jnp.sum(reward, axis=1, keepdims=True)
    second = jnp.sum(reward * reward, axis=1, keepdims=True)
    sizes = jnp.zeros((games, LANES), jnp.int32)
    held = [jnp.zeros((games, LANES), jnp.float32) for _ in range(CAP)]
    for t in range(games):
        begin, size = start_of[t], length_of[t]
        sizes = jnp.where(trainer == t, size, sizes)
        parts = []
        for j in range(CAP):
            part = wide_ref[pl.ds(begin + j, across, stride=stride), :]
            scale = scale_ref[pl.ds(begin + j, 1), :]
            parts.append(jnp.where(j < size, part * scale * gain, 0.0))
            value = reward_at[0, jnp.minimum(begin + j, row_count - 1)]
            held[j] = jnp.where(trainer == t, value, held[j])
        block = jnp.concatenate(parts, axis=0).astype(jnp.bfloat16)
        target = of_group([place_of[t * groups + group] for group in range(groups)], mine)
        out_ref[target, :last] = block.reshape(last, PAIR, LANES)

    own = place - CAP * actor
    kept = (own >= 0) & (own < sizes)
    values = jnp.where(place == slots, first, jnp.where(place == slots + 1, second, 0.0))
    values = jnp.where(place == slots + 2, sizes.astype(jnp.float32), values)
    for j in range(CAP):
        values = jnp.where(kept & (own == j), held[j], values)
    high = values.astype(jnp.bfloat16).astype(jnp.float32)
    middle = (values - high).astype(jnp.bfloat16).astype(jnp.float32)
    low = values - high - middle
    scalar_ref[pl.ds(0, games, stride=PAIR), :] = jnp.where(lane < HALF, high, middle)
    scalar_ref[pl.ds(1, games, stride=PAIR), :] = jnp.where(lane < HALF, low, jnp.where(kept, 1.0, 0.0))
    tiles = scalar_ref[...].astype(jnp.bfloat16).reshape(games, PAIR, LANES)
    for t in range(games):
        for group in range(groups):
            out_ref[place_of[t * groups + group], last] = tiles[t]


def total(in_ref, blocks):
    terms = [in_ref[block, in_ref.shape[1] - 1].astype(jnp.float32) for block in blocks]
    while len(terms) > 1:
        terms = [sum(terms[at : at + 2]) for at in range(0, len(terms), 2)]
    return terms[0]


def sum_kernel(slots, in_ref, every_ref):
    every = total(in_ref, range(in_ref.shape[0]))
    every_ref[...] = jnp.zeros_like(every_ref)
    for n in range(3):
        at = slots + n
        parts = (every[:1, at : at + 1], every[:1, HALF + at : HALF + at + 1], every[1:, at : at + 1])
        high, middle, low = (jnp.broadcast_to(part, (1, LANES)) for part in parts)
        every_ref[n : n + 1] = high + middle + low


def rows_kernel(place_of, groups, in_ref, rows_ref, own_ref, piece_ref):
    actors = in_ref.shape[0] // groups
    last = in_ref.shape[1] - 1
    slots, width = rows_ref.shape
    across = width // LANES
    mine = lax.axis_index("rep") // PARTS
    own_places = [of_group(place_of[s * groups : (s + 1) * groups], mine) for s in range(actors)]
    for s, at in enumerate(own_places):
        block = in_ref[at, :last].reshape(last * PAIR, LANES).astype(jnp.float32)
        piece_ref[s * last * PAIR : (s + 1) * last * PAIR] = block
    for k in range(across):
        lanes = piece_ref[pl.ds(k, slots, stride=across), :]
        rows_ref[:, k * LANES : (k + 1) * LANES] = lanes.astype(jnp.bfloat16)
    own = total(in_ref, own_places)
    own_ref[...] = jnp.zeros_like(own_ref)
    own_ref[:1, :HALF] = own[:1, :HALF] + own[:1, HALF:] + own[1:, :HALF]
    own_ref[1:2, :HALF] = own[1:, HALF:]


def reward_kernel(rows_total, every_ref, other_ref, own_ref, reward_ref, count_ref):
    slots = reward_ref.shape[1]
    every = every_ref[...] + other_ref[...]
    mean, second = every[:1] / rows_total, every[1:2] / rows_total
    scale = lax.rsqrt(second - mean * mean + EPS_VAR)
    scaled = jnp.where(own_ref[1:2] > 0.5, (own_ref[:1] - mean) * scale, 0.0)
    reward_ref[...] = scaled[:, :slots]
    count_ref[...] = every[2:3, :1].astype(jnp.int32)


def fused(features, rewards, lengths, owners, norm_gain):
    row_count, width = features.shape[2:]
    games = lengths.shape[2]
    actors, groups = lax.axis_size("actors"), lax.axis_size("rep")
    slots = actors * CAP
    across = width // LANES
    last = CAP * across // PAIR
    parts, place_of = places(actors, groups)
    inner = groups // PARTS
    tile = jax.ShapeDtypeStruct((SUBLANES, LANES), jnp.float32)
    params = pltpu.CompilerParams(vmem_limit_bytes=VMEM_GRANT)
    vmem = pl.BlockSpec(memory_space=pltpu.VMEM)
    smem = pl.BlockSpec(memory_space=pltpu.SMEM)
    packed = pl.pallas_call(
        functools.partial(pack_kernel, place_of, inner),
        out_shape=jax.ShapeDtypeStruct((games * inner, last + 1, PAIR, LANES), jnp.bfloat16),
        in_specs=[smem, smem, smem, vmem, vmem, vmem],
        out_specs=vmem,
        scratch_shapes=[
            pltpu.VMEM(((across + 1) * row_count, LANES), jnp.float32),
            pltpu.VMEM((row_count + SUBLANES, LANES), jnp.float32),
            pltpu.VMEM((PAIR * games, LANES), jnp.float32),
            pltpu.SMEM((games,), jnp.int32),
            pltpu.SMEM((games,), jnp.int32),
        ],
        compiler_params=params,
        name="pack",
    )(
        *(
            pltpu.with_memory_space_constraint(x, pltpu.HBM)
            for x in (
                lengths.reshape(1, games),
                owners.reshape(1, games),
                rewards.reshape(1, row_count),
                features.reshape(row_count, width),
                norm_gain.reshape(across, LANES),
                rewards.reshape(1, row_count),
            )
        )
    )
    landed = lax.all_to_all(
        packed, ("actors", "rep"), split_axis=0, concat_axis=0, tiled=True, axis_index_groups=parts
    )
    every = pl.pallas_call(
        functools.partial(sum_kernel, slots),
        out_shape=tile,
        in_specs=[vmem],
        out_specs=vmem,
        compiler_params=params,
        name="sums",
    )(landed)
    others = [(group, group // PARTS * PARTS + (group + 1) % PARTS) for group in range(groups)]
    other = lax.ppermute(every, "rep", others)
    rows, own = pl.pallas_call(
        functools.partial(rows_kernel, place_of, inner),
        out_shape=(jax.ShapeDtypeStruct((slots, width), jnp.bfloat16), tile),
        in_specs=[vmem],
        out_specs=(vmem, vmem),
        scratch_shapes=[pltpu.VMEM((slots * across, LANES), jnp.float32)],
        compiler_params=params,
        name="rows",
    )(landed)
    scaled, count = pl.pallas_call(
        functools.partial(reward_kernel, row_count * actors * groups),
        out_shape=(jax.ShapeDtypeStruct((1, slots), jnp.float32), jax.ShapeDtypeStruct((1, 1), jnp.int32)),
        in_specs=[vmem, vmem, vmem],
        out_specs=(vmem, vmem),
        compiler_params=params,
        name="rewards",
    )(every, other, own)
    return (rows.reshape(1, 1, -1, width), scaled.reshape(1, 1, -1), count.reshape(1))


def rms_scale(rows, norm_gain):
    widened = rows.astype(jnp.float32)
    square_mean = jnp.mean(widened * widened, axis=-1, keepdims=True)
    return (widened * lax.rsqrt(square_mean + EPS_NORM) * norm_gain).astype(jnp.bfloat16)


def plain(features, rewards, lengths, owners, norm_gain):
    rows_here = features[0, 0]
    reward_here = rewards[0, 0]
    game_len = lengths[0, 0]
    game_owner = owners[0, 0]
    games = game_len.shape[0]
    row_count = rows_here.shape[0]
    width = rows_here.shape[1]
    row_total = row_count * lax.axis_size("actors") * lax.axis_size("rep")
    starts = jnp.cumsum(game_len) - game_len
    trainer_ids = jnp.arange(games, dtype=jnp.int32)
    owns_game = (game_owner[None, :] == trainer_ids[:, None]).astype(jnp.int32)
    held_len = jnp.sum(owns_game * game_len[None, :], axis=1)
    held_start = jnp.sum(owns_game * starts[None, :], axis=1)
    slot_pos = jnp.arange(CAP, dtype=jnp.int32)
    usable = slot_pos[None, :] < held_len[:, None]
    row_index = jnp.minimum(held_start[:, None] + slot_pos[None, :], row_count - 1)
    outgoing = jnp.where(usable, jnp.take(reward_here, row_index, axis=0), jnp.zeros((), jnp.float32))
    outgoing = jnp.concatenate([outgoing, held_len.astype(jnp.float32)[:, None]], axis=1)
    arrived = lax.all_to_all(outgoing, "actors", split_axis=0, concat_axis=0, tiled=True)
    arrived, arrived_len = arrived[:, :CAP], arrived[:, CAP:]
    normed = rms_scale(rows_here, norm_gain)
    packed = jnp.where(usable[:, :, None], jnp.take(normed, row_index, axis=0), jnp.zeros((), jnp.bfloat16))
    landed = lax.all_to_all(packed, "actors", split_axis=0, concat_axis=0, tiled=True)
    first, second = lax.psum((jnp.sum(arrived), jnp.sum(arrived * arrived)), ("actors", "rep"))
    reward_mean = first / row_total
    inv_spread = lax.rsqrt(second / row_total - reward_mean * reward_mean + EPS_VAR)
    keep_slot = slot_pos[None, :].astype(jnp.float32) < arrived_len
    scaled = jnp.where(keep_slot, (arrived - reward_mean) * inv_spread, jnp.zeros((), jnp.float32))
    count_here = jnp.sum(arrived_len).astype(jnp.int32)
    counts = lax.psum(count_here, "rep")
    return (landed.reshape(1, 1, -1, width), scaled.reshape(1, 1, -1), counts.reshape(1))


def local(features, rewards, lengths, owners, norm_gain):
    actors, groups = lax.axis_size("actors"), lax.axis_size("rep")
    row_count, width = features.shape[2:]
    fits = (
        actors * CAP + 3 <= HALF
        and lengths.shape[2] == actors
        and groups % PARTS == 0
        and actors % SUBLANES == 0
        and width % (SUBLANES * LANES) == 0
        and row_count % 16 == 0
        and row_count <= LANES
    )
    step = fused if fits else plain
    return step(features, rewards, lengths, owners, norm_gain)


def solution(mesh):
    return jax.shard_map(
        local,
        mesh=mesh,
        in_specs=(
            P("rep", "actors", None, None),
            P("rep", "actors", None),
            P("rep", "actors", None),
            P("rep", "actors", None),
            P(),
        ),
        out_specs=(P("rep", "actors", None, None), P("rep", "actors", None), P("actors")),
        check_vma=False,
    )
```

```python
import functools

import jax
import jax.numpy as jnp
from jax import lax
from jax.experimental import pallas as pl
from jax.experimental.pallas import tpu as pltpu
from jax.sharding import PartitionSpec as P

CAP = 3
EPS_NORM = 1e-06
EPS_VAR = 1e-05

LANES = 128
SUBLANES = 8
PAIR = 2
HALF = LANES // 2
VMEM_GRANT = 8 << 20
PARTS = 2
ORDERS = {(8, 4): [11, 7, 6, 3, 8, 4, 15, 14, 12, 10, 2, 0, 1, 5, 9, 13]}


def places(actors, groups):
    inner = groups // PARTS
    order = ORDERS.get((actors, groups)) or [a * inner + g for g in range(inner) for a in range(actors)]
    parts = [[d // inner * groups + d % inner * PARTS + part for d in order] for part in range(PARTS)]
    return parts, [order.index(device) for device in range(actors * inner)]


def of_group(choices, mine):
    chosen = jnp.int32(choices[0])
    for group in range(1, len(choices)):
        chosen = jnp.where(mine == group, choices[group], chosen)
    return chosen


def pack_kernel(
    place_of, groups, length_ref, owner_ref, reward_at, rows_ref, gain_ref, reward_ref,
    out_ref, normed_ref, scalar_ref, start_of, length_of,
):
    games = length_ref.shape[1]
    row_count, width = rows_ref.shape
    across = width // LANES
    stride = row_count
    last = out_ref.shape[1] - 1
    mine, actor = lax.axis_index("rep") // PARTS, lax.axis_index("actors")
    slots = lax.axis_size("actors") * CAP

    start = jnp.int32(0)
    for game in range(games):
        owner, size = owner_ref[0, game], length_ref[0, game]
        start_of[owner] = start
        length_of[owner] = size
        start = start + size

    wide = rows_ref[...].astype(jnp.float32)
    square_mean = jnp.sum(wide * wide, axis=1, keepdims=True) / width
    normed = wide * lax.rsqrt(square_mean + EPS_NORM) * gain_ref[...]
    for k in range(across):
        normed_ref[k * stride : k * stride + row_count] = normed[:, k * LANES : (k + 1) * LANES]

    lane = lax.broadcasted_iota(jnp.int32, (games, LANES), 1)
    place = lane % HALF
    trainer = lax.broadcasted_iota(jnp.int32, (games, LANES), 0)
    reward = reward_ref[...]
    first = jnp.sum(reward, axis=1, keepdims=True)
    second = jnp.sum(reward * reward, axis=1, keepdims=True)
    sizes = jnp.zeros((games, LANES), jnp.int32)
    held = [jnp.zeros((games, LANES), jnp.float32) for _ in range(CAP)]
    for t in range(games):
        begin, size = start_of[t], length_of[t]
        sizes = jnp.where(trainer == t, size, sizes)
        parts = []
        for j in range(CAP):
            part = normed_ref[pl.ds(begin + j, across, stride=stride), :]
            parts.append(jnp.where(j < size, part, 0.0))
            value = reward_at[0, jnp.minimum(begin + j, row_count - 1)]
            held[j] = jnp.where(trainer == t, value, held[j])
        block = jnp.concatenate(parts, axis=0).astype(jnp.bfloat16)
        target = of_group([place_of[t * groups + group] for group in range(groups)], mine)
        out_ref[target, :last] = block.reshape(last, PAIR, LANES)

    own = place - CAP * actor
    kept = (own >= 0) & (own < sizes)
    values = jnp.where(place == slots, first, jnp.where(place == slots + 1, second, 0.0))
    values = jnp.where(place == slots + 2, sizes.astype(jnp.float32), values)
    for j in range(CAP):
        values = jnp.where(kept & (own == j), held[j], values)
    high = values.astype(jnp.bfloat16).astype(jnp.float32)
    middle = (values - high).astype(jnp.bfloat16).astype(jnp.float32)
    low = values - high - middle
    scalar_ref[pl.ds(0, games, stride=PAIR), :] = jnp.where(lane < HALF, high, middle)
    scalar_ref[pl.ds(1, games, stride=PAIR), :] = jnp.where(lane < HALF, low, jnp.where(kept, 1.0, 0.0))
    tiles = scalar_ref[...].astype(jnp.bfloat16).reshape(games, PAIR, LANES)
    for t in range(games):
        for group in range(groups):
            out_ref[place_of[t * groups + group], last] = tiles[t]


def total(in_ref, blocks):
    terms = [in_ref[block, in_ref.shape[1] - 1].astype(jnp.float32) for block in blocks]
    while len(terms) > 1:
        terms = [sum(terms[at : at + 2]) for at in range(0, len(terms), 2)]
    return terms[0]


def sum_kernel(slots, in_ref, every_ref):
    every = total(in_ref, range(in_ref.shape[0]))
    every_ref[...] = jnp.zeros_like(every_ref)
    for n in range(3):
        at = slots + n
        parts = (every[:1, at : at + 1], every[:1, HALF + at : HALF + at + 1], every[1:, at : at + 1])
        high, middle, low = (jnp.broadcast_to(part, (1, LANES)) for part in parts)
        every_ref[n : n + 1] = high + middle + low


def rows_kernel(place_of, groups, in_ref, rows_ref, own_ref, piece_ref):
    actors = in_ref.shape[0] // groups
    last = in_ref.shape[1] - 1
    slots, width = rows_ref.shape
    across = width // LANES
    mine = lax.axis_index("rep") // PARTS
    own_places = [of_group(place_of[s * groups : (s + 1) * groups], mine) for s in range(actors)]
    for s, at in enumerate(own_places):
        block = in_ref[at, :last].reshape(last * PAIR, LANES).astype(jnp.float32)
        piece_ref[s * last * PAIR : (s + 1) * last * PAIR] = block
    for k in range(across):
        lanes = piece_ref[pl.ds(k, slots, stride=across), :]
        rows_ref[:, k * LANES : (k + 1) * LANES] = lanes.astype(jnp.bfloat16)
    own = total(in_ref, own_places)
    own_ref[...] = jnp.zeros_like(own_ref)
    own_ref[:1, :HALF] = own[:1, :HALF] + own[:1, HALF:] + own[1:, :HALF]
    own_ref[1:2, :HALF] = own[1:, HALF:]


def reward_kernel(rows_total, every_ref, other_ref, own_ref, reward_ref, count_ref):
    slots = reward_ref.shape[1]
    every = every_ref[...] + other_ref[...]
    mean, second = every[:1] / rows_total, every[1:2] / rows_total
    scale = lax.rsqrt(second - mean * mean + EPS_VAR)
    scaled = jnp.where(own_ref[1:2] > 0.5, (own_ref[:1] - mean) * scale, 0.0)
    reward_ref[...] = scaled[:, :slots]
    count_ref[...] = every[2:3, :1].astype(jnp.int32)


def fused(features, rewards, lengths, owners, norm_gain):
    row_count, width = features.shape[2:]
    games = lengths.shape[2]
    actors, groups = lax.axis_size("actors"), lax.axis_size("rep")
    slots = actors * CAP
    across = width // LANES
    last = CAP * across // PAIR
    parts, place_of = places(actors, groups)
    inner = groups // PARTS
    tile = jax.ShapeDtypeStruct((2 * PAIR, LANES), jnp.float32)
    params = pltpu.CompilerParams(vmem_limit_bytes=VMEM_GRANT)
    vmem = pl.BlockSpec(memory_space=pltpu.VMEM)
    smem = pl.BlockSpec(memory_space=pltpu.SMEM)
    packed = pl.pallas_call(
        functools.partial(pack_kernel, place_of, inner),
        out_shape=jax.ShapeDtypeStruct((games * inner, last + 1, PAIR, LANES), jnp.bfloat16),
        in_specs=[smem, smem, smem, vmem, vmem, vmem],
        out_specs=vmem,
        scratch_shapes=[
            pltpu.VMEM(((across + 1) * row_count, LANES), jnp.float32),
            pltpu.VMEM((PAIR * games, LANES), jnp.float32),
            pltpu.SMEM((games,), jnp.int32),
            pltpu.SMEM((games,), jnp.int32),
        ],
        compiler_params=params,
        name="pack",
    )(
        *(
            pltpu.with_memory_space_constraint(x, pltpu.HBM)
            for x in (
                lengths.reshape(1, games),
                owners.reshape(1, games),
                rewards.reshape(1, row_count),
                features.reshape(row_count, width),
                norm_gain.reshape(1, width),
                rewards.reshape(1, row_count),
            )
        )
    )
    landed = lax.all_to_all(
        packed, ("actors", "rep"), split_axis=0, concat_axis=0, tiled=True, axis_index_groups=parts
    )
    every = pl.pallas_call(
        functools.partial(sum_kernel, slots),
        out_shape=tile,
        in_specs=[vmem],
        out_specs=vmem,
        compiler_params=params,
        name="sums",
    )(landed)
    others = [(group, group // PARTS * PARTS + (group + 1) % PARTS) for group in range(groups)]
    other = lax.ppermute(every, "rep", others)
    rows, own = pl.pallas_call(
        functools.partial(rows_kernel, place_of, inner),
        out_shape=(jax.ShapeDtypeStruct((slots, width), jnp.bfloat16), tile),
        in_specs=[vmem],
        out_specs=(vmem, vmem),
        scratch_shapes=[pltpu.VMEM((slots * across, LANES), jnp.float32)],
        compiler_params=params,
        name="rows",
    )(landed)
    scaled, count = pl.pallas_call(
        functools.partial(reward_kernel, row_count * actors * groups),
        out_shape=(jax.ShapeDtypeStruct((1, slots), jnp.float32), jax.ShapeDtypeStruct((1, 1), jnp.int32)),
        in_specs=[vmem, vmem, vmem],
        out_specs=(vmem, vmem),
        compiler_params=params,
        name="rewards",
    )(every, other, own)
    return (rows.reshape(1, 1, -1, width), scaled.reshape(1, 1, -1), count.reshape(1))


def rms_scale(rows, norm_gain):
    widened = rows.astype(jnp.float32)
    square_mean = jnp.mean(widened * widened, axis=-1, keepdims=True)
    return (widened * lax.rsqrt(square_mean + EPS_NORM) * norm_gain).astype(jnp.bfloat16)


def plain(features, rewards, lengths, owners, norm_gain):
    rows_here = features[0, 0]
    reward_here = rewards[0, 0]
    game_len = lengths[0, 0]
    game_owner = owners[0, 0]
    games = game_len.shape[0]
    row_count = rows_here.shape[0]
    width = rows_here.shape[1]
    row_total = row_count * lax.axis_size("actors") * lax.axis_size("rep")
    starts = jnp.cumsum(game_len) - game_len
    trainer_ids = jnp.arange(games, dtype=jnp.int32)
    owns_game = (game_owner[None, :] == trainer_ids[:, None]).astype(jnp.int32)
    held_len = jnp.sum(owns_game * game_len[None, :], axis=1)
    held_start = jnp.sum(owns_game * starts[None, :], axis=1)
    slot_pos = jnp.arange(CAP, dtype=jnp.int32)
    usable = slot_pos[None, :] < held_len[:, None]
    row_index = jnp.minimum(held_start[:, None] + slot_pos[None, :], row_count - 1)
    outgoing = jnp.where(usable, jnp.take(reward_here, row_index, axis=0), jnp.zeros((), jnp.float32))
    outgoing = jnp.concatenate([outgoing, held_len.astype(jnp.float32)[:, None]], axis=1)
    arrived = lax.all_to_all(outgoing, "actors", split_axis=0, concat_axis=0, tiled=True)
    arrived, arrived_len = arrived[:, :CAP], arrived[:, CAP:]
    normed = rms_scale(rows_here, norm_gain)
    packed = jnp.where(usable[:, :, None], jnp.take(normed, row_index, axis=0), jnp.zeros((), jnp.bfloat16))
    landed = lax.all_to_all(packed, "actors", split_axis=0, concat_axis=0, tiled=True)
    first, second = lax.psum((jnp.sum(arrived), jnp.sum(arrived * arrived)), ("actors", "rep"))
    reward_mean = first / row_total
    inv_spread = lax.rsqrt(second / row_total - reward_mean * reward_mean + EPS_VAR)
    keep_slot = slot_pos[None, :].astype(jnp.float32) < arrived_len
    scaled = jnp.where(keep_slot, (arrived - reward_mean) * inv_spread, jnp.zeros((), jnp.float32))
    count_here = jnp.sum(arrived_len).astype(jnp.int32)
    counts = lax.psum(count_here, "rep")
    return (landed.reshape(1, 1, -1, width), scaled.reshape(1, 1, -1), counts.reshape(1))


def local(features, rewards, lengths, owners, norm_gain):
    actors, groups = lax.axis_size("actors"), lax.axis_size("rep")
    row_count, width = features.shape[2:]
    fits = (
        actors * CAP + 3 <= HALF
        and lengths.shape[2] == actors
        and groups % PARTS == 0
        and actors % SUBLANES == 0
        and width % (SUBLANES * LANES) == 0
        and row_count % 16 == 0
        and row_count <= LANES
    )
    step = fused if fits else plain
    return step(features, rewards, lengths, owners, norm_gain)


def solution(mesh):
    return jax.shard_map(
        local,
        mesh=mesh,
        in_specs=(
            P("rep", "actors", None, None),
            P("rep", "actors", None),
            P("rep", "actors", None),
            P("rep", "actors", None),
            P(),
        ),
        out_specs=(P("rep", "actors", None, None), P("rep", "actors", None), P("actors")),
        check_vma=False,
    )
```
